256 devices in a mesh: samp: 64 (over y, z, core), tile: 4 (over x).
Axes of the slice: x: 4, y: 4, z: 8, core: 2. Of those that a mesh axis runs over, the one named last changes fastest.
Arguments:
- features: bfloat16 [256, 48, 48, 256], P(('samp', 'tile')), may hold values from -24 to 24
- spin_words: int32 [256, 77], P(('samp', 'tile')), may hold values from 0 to 1073741823
- conv_weight: bfloat16 [256, 224], replicated, may hold values from -0.375 to 0.375
- spin_bias: float32 [256], replicated, may hold values from -4 to 4
- readout: float32 [256], replicated, may hold values from -0.41 to 0.41
- sector: int32 [1], replicated, may hold values from 0 to 2303
- diag_shift: float32 [1], replicated, may hold values from 0.01 to 0.3
- energy_dev: float32 [256], P(('samp', 'tile')), may hold values from -6 to 6
Outputs:
- update: float32 [256, 224], P(('samp', 'tile'))
The draws below stay inside these ranges and needn't reach their ends.
All inputs are finite; a program needn't handle non-finite values.
Results may differ from the reference program's by a relative error of at most 0.0052.
Values may be sent and summed in bfloat16 or wider, within the bound.
A program may use at most 64 MiB of HBM per device.

```python
import math
import jax
import jax.numpy as jnp
from jax import lax

SIDE = 48
CH = 256
CI = 32
TAPS = 7
GROUPS = 8
WORDS = 77
SAMPLES = 256


def draw_features(key, part):
    key_sample, key_channel, key_base = jax.random.split(key, 3)
    sample_scale = jnp.power(10.0, jax.random.uniform(key_sample, (SAMPLES, 1, 1, 1), jnp.float32, -0.5, 0.5))
    channel_scale = jnp.power(10.0, jax.random.uniform(key_channel, (1, 1, 1, CH), jnp.float32, -0.25, 0.25))
    base_field = jnp.clip(jax.random.normal(key_base, (SAMPLES, SIDE, SIDE, CH), jnp.float32), -4.0, 4.0)
    return (base_field * sample_scale * channel_scale).astype(jnp.bfloat16)


def draw_readout(key, part):
    key_spread, key_sign = jax.random.split(key, 2)
    position = (jnp.arange(CH, dtype=jnp.float32) + jax.random.uniform(key_spread, (CH,), jnp.float32)) / CH
    magnitude = 0.02 * jnp.power(10.0, position)
    sign_draw = jnp.where(jax.random.bernoulli(key_sign, 0.5, (CH,)), 1.0, -1.0)
    return (magnitude * sign_draw).astype(jnp.float32)


def with_ends(entries, stream_key, smallest, high):
    extent = entries.shape
    spot = [jax.random.randint(jax.random.fold_in(stream_key, axis), (), 0, extent[axis]) for axis in range(len(extent))]
    entries = entries.at[tuple(spot)].set(smallest)
    longest = extent.index(max(extent))
    spot[longest] = (spot[longest] + 1) % extent[longest]
    return entries.at[tuple(spot)].set(high)


def block_scale(stream_key, dims, cuts, low, high):
    level, own = 1.0, jax.random.fold_in(stream_key, 6)
    for dim, shards_of in cuts:
        draws = jnp.exp(jax.random.uniform(jax.random.fold_in(own, dim), (shards_of,), jnp.float32, low / len(cuts), high / len(cuts)))
        level = level * jnp.repeat(draws, dims[dim] // shards_of).reshape([-1 if axis == dim else 1 for axis in range(len(dims))])
    return level


def bell_draw(own_key, shape, width, reach, pieces=(), kind=jnp.bfloat16):
    entries = width * jax.random.normal(own_key, shape, jnp.float32)
    if pieces:
        entries = entries * block_scale(own_key, shape, pieces, -0.22, 0.18)
    return jnp.clip(entries, -reach, reach).astype(kind)


def setup_inputs(seed: int = 0) -> dict:
    keys = jax.random.split(jax.random.key(seed), 9)
    features = draw_features(jax.random.fold_in(keys[8], 71), 0)
    spin_words = with_ends(jax.random.randint(keys[1], (SAMPLES, WORDS), 0, 2 ** 30), jax.random.fold_in(keys[1], 1), 0, (2 ** 30) - 1).astype(jnp.int32)
    conv_weight = bell_draw(keys[2], (CH, TAPS * CI), (TAPS * CI) ** -0.5, 0.375)
    spin_bias = bell_draw(keys[3], (CH,), 1.0, 4.0, (), jnp.float32)
    readout = draw_readout(jax.random.fold_in(keys[8], 71), 0)
    sector = jax.random.randint(keys[5], (1,), 0, SIDE * SIDE).astype(jnp.int32)
    diag_shift = jnp.clip(jnp.exp(jax.random.uniform(keys[6], (1,), jnp.float32, math.log(0.01), math.log(0.3))), 0.01, 0.3)
    energy_dev = bell_draw(keys[7], (SAMPLES,), 1.0, 6.0, ((0, 256),), jnp.float32)
    return {"features": features, "spin_words": spin_words, "conv_weight": conv_weight, "spin_bias": spin_bias, "readout": readout, "sector": sector, "diag_shift": diag_shift, "energy_dev": energy_dev}


OFFSETS = ((0, 0), (1, 0), (-1, 0), (0, 1), (0, -1), (1, -1), (-1, 1))

def cholesky_solve(factor, target):
    column = target[:, None]
    middle = lax.linalg.triangular_solve(factor, column, left_side=True, lower=True)
    result = lax.linalg.triangular_solve(factor, middle, left_side=True, lower=True, transpose_a=True)
    return result[:, 0]

def unpack_spins(spin_words, side):
    bit_index = jnp.arange(30, dtype=jnp.int32)
    flat_bits = spin_words[:, :, None] >> bit_index[None, None, :] & 1
    flat_bits = flat_bits.reshape(spin_words.shape[0], -1)[:, :side * side]
    return (2 * flat_bits - 1).astype(jnp.float32).reshape(spin_words.shape[0], side, side)

def phase_table(sector, side):
    wave_row = sector[0] // side
    wave_col = sector[0] % side
    coords = jnp.arange(side, dtype=jnp.int32)
    wave_arg = (wave_row * coords[:, None] + wave_col * coords[None, :]) % side
    return jnp.cos(2.0 * math.pi / side * wave_arg.astype(jnp.float32))

def sample_rows(feature, spin_sign, kernel, spin_bias, readout, phase_field):
    patches = jnp.stack([jnp.roll(feature, (-di, -dj), (0, 1)) for di, dj in OFFSETS], axis=2)
    patches = patches.reshape(SIDE * SIDE, TAPS, GROUPS, CI).astype(jnp.float32)
    preact = jnp.einsum('nkgi,goki->ngo', patches, kernel.astype(jnp.float32))
    preact = preact + spin_bias.reshape(GROUPS, CI)[None] * spin_sign.reshape(-1)[:, None, None]
    logistic = jax.nn.sigmoid(preact)
    cotangent = phase_field.reshape(-1)[:, None, None] * readout.reshape(GROUPS, CI)[None]
    cotangent = (cotangent * logistic * (1.0 + preact * (1.0 - logistic))).astype(jnp.bfloat16)
    log_deriv = jnp.einsum('ngo,nkgi->goki', cotangent.astype(jnp.float32), patches)
    return log_deriv.reshape(CH, TAPS * CI).astype(jnp.bfloat16)

def reference(features, spin_words, conv_weight, spin_bias, readout, sector, diag_shift, energy_dev):
    spin_sign = unpack_spins(spin_words, SIDE)
    phase_field = phase_table(sector, SIDE)
    kernel = conv_weight.reshape(GROUPS, CI, TAPS, CI)

    def one_sample(pair):
        return sample_rows(pair[0], pair[1], kernel, spin_bias, readout, phase_field)
    log_deriv = lax.map(one_sample, (features, spin_sign))
    widened = log_deriv.reshape(SAMPLES, CH * TAPS * CI).astype(jnp.float32)
    centered = (widened - lax.optimization_barrier(jnp.mean(widened, axis=0, keepdims=True))) / math.sqrt(SAMPLES)
    gram_matrix = jnp.dot(centered, centered.T, precision=lax.Precision.HIGHEST)
    shift_value = diag_shift[0] * jnp.trace(gram_matrix) / SAMPLES
    factor = jnp.linalg.cholesky(gram_matrix + shift_value * jnp.eye(SAMPLES, dtype=jnp.float32))
    solved = cholesky_solve(factor, energy_dev)
    raw_step = jnp.dot(solved, centered, precision=lax.Precision.HIGHEST)
    mean_square = jnp.mean(raw_step * raw_step)
    update = -raw_step / jnp.sqrt(mean_square + 1e-06)
    return update.reshape(CH, TAPS * CI)
```

```python
import functools
import math

import jax
import jax.numpy as jnp
from jax import lax
from jax.experimental import pallas as pl
from jax.experimental.pallas import tpu as pltpu
from jax.sharding import PartitionSpec as P

SIDE = 48
SITES = SIDE * SIDE
PAD = SITES + 2 * SIDE
CH = 256
CI = 32
TAPS = 7
PARAMS = CH * TAPS * CI
NS = 256
G = 16

SOURCES = ((0, 0), (0, 1), (0, -1), (1, 0), (2, 0), (2, 1), (1, -1))
TILE = 256
F32 = jnp.float32
BF16 = jnp.bfloat16
HIGHEST = lax.Precision.HIGHEST


def iota(shape, dim):
    return lax.broadcasted_iota(jnp.int32, shape, dim)


def column_of(row):
    shape = (CH, CH)
    picked = jnp.where(iota(shape, 0) == iota(shape, 1), jnp.broadcast_to(row, shape), 0.0)
    return jnp.sum(picked, axis=1, keepdims=True)


def local_kernel(
    words_ref, sector_ref, energy_ref, w_ref, bias_ref, readout_ref, feat_ref,
    out_ref, f0, fp, fm, wb, cot, word_row, sems,
):
    copies = (
        pltpu.make_async_copy(feat_ref, f0.at[pl.ds(SIDE, SITES)], sems.at[0]),
        pltpu.make_async_copy(feat_ref.at[pl.ds(SITES - SIDE, SIDE)], f0.at[pl.ds(0, SIDE)], sems.at[1]),
        pltpu.make_async_copy(feat_ref.at[pl.ds(0, SIDE)], f0.at[pl.ds(SIDE + SITES, SIDE)], sems.at[2]),
    )
    for copy in copies:
        copy.start()

    weight = w_ref[...]
    same = (iota((CH, CH), 0) // CI) == (iota((CH, CH), 1) // CI)
    source_row = iota((TAPS * CI, CH), 0)
    lane_in = iota((TAPS * CI, CH), 1) % CI
    for k in range(TAPS):
        spread = (source_row == lane_in + k * CI).astype(F32).astype(BF16)
        block = jnp.dot(weight, spread, preferred_element_type=F32)
        wb[k] = jnp.where(same, block, 0.0).astype(BF16)

    word_row[...] = jnp.zeros_like(word_row)
    word_row[:, 0:77] = words_ref[...]
    bits = (jnp.broadcast_to(word_row[...], (32, 128)) >> iota((32, 128), 0)) & 1
    bits = bits.astype(F32).astype(BF16)
    site = iota((1, SITES), 1)
    word_of = site // 30
    bit_of = site - 30 * word_of
    pick_word = (iota((128, SITES), 0) == jnp.broadcast_to(word_of, (128, SITES))).astype(F32).astype(BF16)
    spread_bits = jnp.dot(bits, pick_word, preferred_element_type=F32)
    pick_bit = iota((32, SITES), 0) == jnp.broadcast_to(bit_of, (32, SITES))
    sign = 2.0 * jnp.sum(jnp.where(pick_bit, spread_bits, 0.0), axis=0, keepdims=True) - 1.0

    sector = sector_ref[0]
    wave_row = sector // SIDE
    wave_col = sector - wave_row * SIDE
    site_i = site // SIDE
    site_j = site - SIDE * site_i
    wave_arg = (wave_row * site_i + wave_col * site_j) % SIDE
    phase = jnp.cos(2.0 * math.pi / SIDE * wave_arg.astype(F32))

    bias = column_of(bias_ref[...])
    readout = column_of(readout_ref[...])

    for copy in copies:
        copy.wait()
    for row in range(SIDE + 2):
        rows = pl.ds(row * SIDE, SIDE)
        wide = f0[rows, :].astype(F32)
        fp[rows, :] = pltpu.roll(wide, SIDE - 1, 0).astype(BF16)
        fm[rows, :] = pltpu.roll(wide, 1, 0).astype(BF16)

    held = (f0, fp, fm)
    for t in range(SITES // TILE):
        start = t * TILE
        preact = bias * sign[:, start : start + TILE]
        for k, (which, shift) in enumerate(SOURCES):
            patch = held[which][pl.ds(SIDE + start + shift * SIDE, TILE), :]
            preact = preact + lax.dot_general(
                wb[k], patch, (((1,), (1,)), ((), ())), preferred_element_type=F32
            )
        logistic = 0.5 + 0.5 * jnp.tanh(0.5 * preact)
        scale = readout * phase[:, start : start + TILE]
        value = scale * logistic * (1.0 + preact * (1.0 - logistic))
        cot[:, start : start + TILE] = value.astype(BF16)

    group = iota((CH, CH), 0) // CI
    lane = iota((CH, CH), 1)
    spare = lane - CI * ((group + TAPS) % 8)
    energy = jnp.full((CH, CH), energy_ref[0], F32)
    high = energy.astype(BF16).astype(F32)
    middle = (energy - high).astype(BF16).astype(F32)
    low = energy - high - middle
    total = jnp.where(spare == 0, high, jnp.where(spare == 1, middle, jnp.where(spare == 2, low, 0.0)))
    for k, (which, shift) in enumerate(SOURCES):
        patch = held[which][pl.ds(SIDE + shift * SIDE, SITES), :]
        block = jnp.dot(cot[...], patch, preferred_element_type=F32)
        block = jnp.where(same, block, 0.0)
        if k:
            block = pltpu.roll(block, k * CI, 1)
        total = total + block
    out_ref[...] = total.astype(BF16)


def local_rows(features, spin_words, conv_weight, spin_bias, readout, sector, energy_dev):
    vmem = pl.BlockSpec(memory_space=pltpu.VMEM)
    smem = pl.BlockSpec(memory_space=pltpu.SMEM)
    return pl.pallas_call(
        local_kernel,
        out_shape=jax.ShapeDtypeStruct((CH, CH), BF16),
        in_specs=[vmem, smem, smem, vmem, vmem, vmem, pl.BlockSpec(memory_space=pl.ANY)],
        out_specs=vmem,
        scratch_shapes=[
            pltpu.VMEM((PAD, CH), BF16),
            pltpu.VMEM((PAD, CH), BF16),
            pltpu.VMEM((PAD, CH), BF16),
            pltpu.VMEM((TAPS, CH, CH), BF16),
            pltpu.VMEM((CH, SITES), BF16),
            pltpu.VMEM((1, 128), jnp.int32),
            pltpu.SemaphoreType.DMA((3,)),
        ],
        compiler_params=pltpu.CompilerParams(vmem_limit_bytes=40 << 20),
        name="local_rows",
    )(
        spin_words, sector, energy_dev, conv_weight,
        spin_bias.reshape(1, CH), readout.reshape(1, CH), features.reshape(SITES, CH),
    )


def exchange_kernel(
    rows_ref, gram_ref, cent_ref, recv1, send2, recv2, part, sums, wide, send_sems, recv_sems
):
    samp = lax.axis_index("samp")
    tile = lax.axis_index("tile")
    h = samp // 4
    l = (samp - h * 4) * 4 + tile
    l_samp = samp - h * 4

    def peer_h(other):
        return (other * 4 + l_samp, tile)

    def peer_l(other):
        other_samp = other // 4
        return (h * 4 + other_samp, other - other_samp * 4)

    barrier = pltpu.get_barrier_semaphore()
    for step in range(1, G):
        pl.semaphore_signal(
            barrier, inc=1, device_id=peer_h(lax.rem(h + step, G)), device_id_type=pl.DeviceIdType.MESH
        )
        pl.semaphore_signal(
            barrier, inc=1, device_id=peer_l(lax.rem(l + step, G)), device_id_type=pl.DeviceIdType.MESH
        )
    pl.semaphore_wait(barrier, 2 * (G - 1))

    def exchange(stage, mine, peer, source, target):
        def send(step, carry):
            other = lax.rem(mine + step, G)
            pltpu.make_async_remote_copy(
                src_ref=source(other),
                dst_ref=target.at[mine],
                send_sem=send_sems.at[stage],
                recv_sem=recv_sems.at[stage],
                device_id=peer(other),
                device_id_type=pl.DeviceIdType.MESH,
            ).start()
            return carry

        lax.fori_loop(1, G, send, 0)

    def finish(stage, target):
        many = target.at[pl.ds(0, G - 1)]
        pltpu.make_async_copy(many, many, recv_sems.at[stage]).wait()
        pltpu.make_async_copy(many, many, send_sems.at[stage]).wait()

    exchange(0, h, peer_h, lambda other: rows_ref.at[other], recv1)
    recv1[h] = rows_ref[h]
    finish(0, recv1)
    turned_row = iota((NS, NS), 0)
    source_row = (turned_row % G) * G + turned_row // G
    turn = (iota((NS, NS), 1) == source_row).astype(F32).astype(BF16)
    turned = jnp.dot(turn, recv1[...].reshape(NS, CH), preferred_element_type=F32)
    send2[...] = turned.astype(BF16).reshape(G, G, CH)
    exchange(1, l, peer_l, lambda other: send2.at[other], recv2)
    recv2[l] = send2[l]
    finish(1, recv2)

    group = samp // 8
    lane = iota((CH, CH), 1)
    order = (iota((CH, CH), 0) == (lane + group * CI) % CH).astype(F32).astype(BF16)
    raw = jnp.dot(recv2[...].reshape(NS, CH), order, preferred_element_type=F32)
    mean = jnp.mean(raw, axis=0, keepdims=True)
    centered = jnp.where(lane < TAPS * CI, (raw - mean) * (1.0 / math.sqrt(NS)), 0.0)
    energy = jnp.sum(jnp.where(lane >= TAPS * CI, raw, 0.0), axis=1, keepdims=True)
    cent_ref[...] = jnp.where(lane == TAPS * CI, energy, centered)
    partial_gram = lax.dot_general(
        centered, centered, (((1,), (1,)), ((), ())), precision=HIGHEST, preferred_element_type=F32
    )
    part[...] = partial_gram.reshape(G, G, NS)

    exchange(2, l, peer_l, lambda other: part.at[other], sums)
    sums[l] = part[l]
    finish(2, sums)
    wide[h] = jnp.sum(sums[...], axis=0)
    exchange(3, h, peer_h, lambda other: wide.at[h], wide)
    finish(3, wide)
    gram_ref[l] = jnp.sum(wide[...], axis=0)
    exchange(4, l, peer_l, lambda other: gram_ref.at[l], gram_ref)
    finish(4, gram_ref)


def exchange_rows(rows):
    vmem = pl.BlockSpec(memory_space=pltpu.VMEM)
    return pl.pallas_call(
        exchange_kernel,
        out_shape=(
            jax.ShapeDtypeStruct((G, G, NS), F32),
            jax.ShapeDtypeStruct((NS, CH), F32),
        ),
        in_specs=[vmem],
        out_specs=(vmem, vmem),
        scratch_shapes=[
            pltpu.VMEM((G, G, CH), BF16),
            pltpu.VMEM((G, G, CH), BF16),
            pltpu.VMEM((G, G, CH), BF16),
            pltpu.VMEM((G, G, NS), F32),
            pltpu.VMEM((G, G, NS), F32),
            pltpu.VMEM((G, G, NS), F32),
            pltpu.SemaphoreType.DMA((5,)),
            pltpu.SemaphoreType.DMA((5,)),
        ],
        compiler_params=pltpu.CompilerParams(
            collective_id=0, has_side_effects=True, vmem_limit_bytes=32 << 20
        ),
        name="exchange_rows",
    )(rows)


def lane_spread(block, index):
    return jnp.take_along_axis(block, index, axis=1)


def solve_kernel(shift_ref, gram_ref, cent_ref, out_ref, work):
    row = iota((NS, NS), 0)
    col = iota((NS, NS), 1)
    gram = gram_ref[...]
    trace = jnp.sum(jnp.where(row == col, gram, 0.0))
    shift = shift_ref[0] * trace / NS
    work[:, 0:NS] = jnp.where(row == col, gram + shift, gram)
    energy_lane = TAPS * CI - 128
    last = cent_ref[:, 128:256]
    work[:, NS : NS + 128] = jnp.where(iota((NS, 128), 1) == energy_lane, last, 0.0)

    sub = iota((8, 128), 0)

    def rows_of(block, j):
        return jnp.broadcast_to(block[j : j + 1, :], (8, 128))

    for half in range(2):
        tiles = range(half, 3)

        def panel_step(kb, carry):
            at = pl.multiple_of(half * 128 + kb * 8, 8)
            own = pl.ds(at, 8)
            panel = [work[own, t * 128 : (t + 1) * 128] for t in tiles]
            index = [jnp.full((8, 128), kb * 8 + c, jnp.int32) for c in range(8)]
            cols = [lane_spread(panel[0], index[c]) for c in range(8)]
            for j in range(8):
                inverse = 1.0 / rows_of(cols[j], j)
                here = sub == j
                for t in range(len(panel)):
                    scaled = rows_of(panel[t], j) * inverse
                    panel[t] = jnp.where(here, scaled, panel[t] - cols[j] * scaled)
                for c in range(j + 1, 8):
                    scaled = rows_of(cols[c], j) * inverse
                    cols[c] = jnp.where(here, scaled, cols[c] - cols[j] * scaled)
            spread = [[rows_of(panel[t], c) for c in range(8)] for t in range(len(panel))]
            for r in range(NS // 8):
                rows = pl.ds(r * 8, 8)
                blocks = [work[rows, t * 128 : (t + 1) * 128] for t in tiles]
                factors = [lane_spread(blocks[0], index[c]) for c in range(8)]
                for t in range(len(panel)):
                    terms = [factors[c] * spread[t][c] for c in range(8)]
                    while len(terms) > 1:
                        terms = [a + b for a, b in zip(terms[::2], terms[1::2])]
                    work[rows, tiles[t] * 128 : (tiles[t] + 1) * 128] = blocks[t] - terms[0]
            for t in range(len(panel)):
                work[own, tiles[t] * 128 : (tiles[t] + 1) * 128] = panel[t]
            return carry

        lax.fori_loop(0, 16, panel_step, 0)

    answer = work[
        :, NS + energy_lane : NS + energy_lane + 1
    ]
    weighted = answer * gram_ref[...]
    product = jnp.sum(weighted, axis=0, keepdims=True)
    answer_row = jnp.sum(jnp.where(row == col, jnp.broadcast_to(answer, (NS, NS)), 0.0), axis=0, keepdims=True)
    square_sum = jnp.sum(product * answer_row, axis=1, keepdims=True)
    raw_step = jnp.sum(answer * cent_ref[...], axis=0, keepdims=True)
    update = -raw_step / jnp.sqrt(square_sum / PARAMS + 1e-06)
    out_ref[...] = update[:, 0 : TAPS * CI]


def solve_update(gram, centered, diag_shift):
    vmem = pl.BlockSpec(memory_space=pltpu.VMEM)
    smem = pl.BlockSpec(memory_space=pltpu.SMEM)
    return pl.pallas_call(
        solve_kernel,
        out_shape=jax.ShapeDtypeStruct((1, TAPS * CI), F32),
        in_specs=[smem, vmem, vmem],
        out_specs=vmem,
        scratch_shapes=[pltpu.VMEM((NS, NS + 128), F32)],
        compiler_params=pltpu.CompilerParams(vmem_limit_bytes=16 << 20),
        name="solve_update",
    )(diag_shift, gram, centered)


def on_device(
    features, spin_words, conv_weight, spin_bias, readout, sector, diag_shift, energy_dev
):
    rows = local_rows(features, spin_words, conv_weight, spin_bias, readout, sector, energy_dev)
    gram, centered = exchange_rows(rows.reshape(G, G, CH))
    return solve_update(gram.reshape(NS, NS), centered, diag_shift)


def solution(mesh):
    placed = (
        P(("samp", "tile"), None, None, None),
        P(("samp", "tile"), None),
        P(),
        P(),
        P(),
        P(),
        P(),
        P(("samp", "tile")),
    )
    return jax.shard_map(
        on_device, mesh=mesh, in_specs=placed, out_specs=P(("samp", "tile"), None), check_vma=False
    )
```

```python
import functools
import math

import jax
import jax.numpy as jnp
from jax import lax
from jax.experimental import pallas as pl
from jax.experimental.pallas import tpu as pltpu
from jax.sharding import PartitionSpec as P

SIDE = 48
SITES = SIDE * SIDE
PAD = SITES + 2 * SIDE
CH = 256
CI = 32
TAPS = 7
PARAMS = CH * TAPS * CI
NS = 256
G = 16

SOURCES = ((0, 0), (0, 1), (0, -1), (1, 0), (2, 0), (2, 1), (1, -1))
TILE = 256
F32 = jnp.float32
BF16 = jnp.bfloat16
HIGHEST = lax.Precision.HIGHEST


def iota(shape, dim):
    return lax.broadcasted_iota(jnp.int32, shape, dim)


def column_of(row):
    shape = (CH, CH)
    picked = jnp.where(iota(shape, 0) == iota(shape, 1), jnp.broadcast_to(row, shape), 0.0)
    return jnp.sum(picked, axis=1, keepdims=True)


def parts_of(value):
    high = value.astype(BF16)
    rest = value - high.astype(F32)
    middle = rest.astype(BF16)
    low = (rest - middle.astype(F32)).astype(BF16)
    return high, middle, low


def row_spread(block, j):
    return jnp.broadcast_to(block[j : j + 1, :], (8, 128))


def lane_spread(block, j):
    return jnp.broadcast_to(block[:, j : j + 1], (8, 128))


def total_of(terms):
    while len(terms) > 1:
        odd = terms[-1:] if len(terms) % 2 else []
        terms = [a + b for a, b in zip(terms[::2], terms[1::2])] + odd
    return terms[0]


def eliminate_panel(panel, base):
    sub = iota((8, 128), 0)
    width = len(panel[0])
    for s in range(4):
        own = list(panel[s])
        cols = [lane_spread(own[0], base + 8 * s + c) for c in range(8)]
        for j in range(8):
            inverse = 1.0 / row_spread(cols[j], j)
            here = sub == j
            for t in range(width):
                scaled = row_spread(own[t], j) * inverse
                own[t] = jnp.where(here, scaled, own[t] - cols[j] * scaled)
            for c in range(j + 1, 8):
                scaled = row_spread(cols[c], j) * inverse
                cols[c] = jnp.where(here, scaled, cols[c] - cols[j] * scaled)
        panel[s] = own
        spread = [[row_spread(own[t], c) for c in range(8)] for t in range(width)]
        for a in range(4):
            if a == s:
                continue
            factors = [lane_spread(panel[a][0], base + 8 * s + c) for c in range(8)]
            panel[a] = [
                panel[a][t] - total_of([factors[c] * spread[t][c] for c in range(8)]) for t in range(width)
            ]
    return panel


def eliminate(work):
    for q in range(NS // 32):
        half, base = q // 4, 32 * (q % 4)
        lanes = [slice(t * 128, (t + 1) * 128) for t in range(half, 3)]
        rows = [slice(q * 32 + 8 * a, q * 32 + 8 * a + 8) for a in range(4)]
        panel = eliminate_panel([[work[r, at] for at in lanes] for r in rows], base)
        solved = jnp.concatenate([jnp.concatenate(group, axis=1) for group in panel], axis=0)
        column = iota((NS, 128), 1)
        factor = work[:, lanes[0]]
        factor = jnp.where((column >= base) & (column < base + 32), factor, 0.0)
        factor = pltpu.roll(factor, (128 - base) % 128, 1) if base else factor
        fh, fm, fl = (part.astype(F32) for part in parts_of(factor))
        left = fh + pltpu.roll(fm, 32, 1) + pltpu.roll(fl, 64, 1)
        left2 = left + pltpu.roll(fh, 96, 1)
        right = fh + pltpu.roll(fm, 32, 1)
        left = jnp.concatenate([left2.astype(BF16), right.astype(BF16)], axis=1)
        mh, mm, ml = (part.astype(F32) for part in parts_of(solved))
        zero = jnp.zeros_like(mh)
        right = jnp.concatenate([mh, mh, mh, mm, ml, mm, zero, zero], axis=0).astype(BF16)
        change = jnp.dot(left, right, preferred_element_type=F32)
        for r in range(NS // 8):
            at_row = slice(r * 8, r * 8 + 8)
            if r // 4 == q:
                for t, at in enumerate(lanes):
                    work[at_row, at] = panel[r % 4][t]
            else:
                for t, at in enumerate(lanes):
                    work[at_row, at] = work[at_row, at] - change[at_row, t * 128 : (t + 1) * 128]


def finish_update(shift_ref, gram_ref, cent_ref, out_ref, work):
    row = iota((NS, NS), 0)
    col = iota((NS, NS), 1)
    gram = gram_ref[...].reshape(NS, NS)
    trace = jnp.sum(jnp.sum(jnp.where(row == col, gram, 0.0), axis=0, keepdims=True), axis=1, keepdims=True)
    shift = shift_ref[0] * (trace * (1.0 / NS))
    work[:, 0:NS] = jnp.where(row == col, gram + shift, gram)
    energy_lane = TAPS * CI - 128
    last = cent_ref[:, 128:256]
    work[:, NS : NS + 128] = jnp.where(iota((NS, 128), 1) == energy_lane, last, 0.0)
    eliminate(work)
    answer = work[:, NS + energy_lane : NS + energy_lane + 1]
    product = jnp.sum(answer * gram_ref[...].reshape(NS, NS), axis=0, keepdims=True)
    answer_row = jnp.sum(jnp.where(row == col, jnp.broadcast_to(answer, (NS, NS)), 0.0), axis=0, keepdims=True)
    square_sum = jnp.sum(product * answer_row, axis=1, keepdims=True)
    raw_step = jnp.sum(answer * cent_ref[...], axis=0, keepdims=True)
    update = -raw_step / jnp.sqrt(square_sum / PARAMS + 1e-06)
    out_ref[...] = update[:, 0 : TAPS * CI]


def local_rows(
    words_ref, sector_ref, energy_ref, w_ref, bias_ref, readout_ref, feature_copies,
    rows_ref, f0, fp, fm, wb, cot, word_row,
):
    weight = w_ref[...]
    same = (iota((CH, CH), 0) // CI) == (iota((CH, CH), 1) // CI)
    source_row = iota((TAPS * CI, CH), 0)
    lane_in = iota((TAPS * CI, CH), 1) % CI
    for k in range(TAPS):
        spread = (source_row == lane_in + k * CI).astype(F32).astype(BF16)
        block = lax.dot_general(weight, spread, (((0,), (0,)), ((), ())), preferred_element_type=F32)
        wb[k] = jnp.where(same, block, 0.0).astype(BF16)

    word_row[...] = jnp.zeros_like(word_row)
    word_row[:, 0:77] = words_ref[...]
    bits = (jnp.broadcast_to(word_row[...], (32, 128)) >> iota((32, 128), 0)) & 1
    bits = bits.astype(F32).astype(BF16)
    site = iota((1, SITES), 1)
    word_of = site // 30
    bit_of = site - 30 * word_of
    pick_word = (iota((128, SITES), 0) == jnp.broadcast_to(word_of, (128, SITES))).astype(F32).astype(BF16)
    spread_bits = jnp.dot(bits, pick_word, preferred_element_type=F32)
    pick_bit = iota((32, SITES), 0) == jnp.broadcast_to(bit_of, (32, SITES))
    sign = 2.0 * jnp.sum(jnp.where(pick_bit, spread_bits, 0.0), axis=0, keepdims=True) - 1.0

    sector = sector_ref[0]
    wave_row = sector // SIDE
    wave_col = sector - wave_row * SIDE
    site_i = site // SIDE
    site_j = site - SIDE * site_i
    wave_arg = (wave_row * site_i + wave_col * site_j) % SIDE
    phase = jnp.cos(2.0 * math.pi / SIDE * wave_arg.astype(F32))

    bias = column_of(bias_ref[...])
    readout = column_of(readout_ref[...])

    for copy in feature_copies:
        copy.wait()
    for row in range(SIDE + 2):
        rows = pl.ds(row * SIDE, SIDE)
        wide = f0[rows, :].astype(F32)
        fp[rows, :] = pltpu.roll(wide, SIDE - 1, 0).astype(BF16)
        fm[rows, :] = pltpu.roll(wide, 1, 0).astype(BF16)

    held = (f0, fp, fm)
    for t in range(SITES // TILE):
        start = t * TILE
        preact = bias * sign[:, start : start + TILE]
        for k, (which, shift) in enumerate(SOURCES):
            patch = held[which][pl.ds(SIDE + start + shift * SIDE, TILE), :]
            preact = preact + lax.dot_general(
                wb[k], patch, (((1,), (1,)), ((), ())), preferred_element_type=F32
            )
        logistic = 0.5 + 0.5 * jnp.tanh(0.5 * preact)
        scale = readout * phase[:, start : start + TILE]
        value = scale * logistic * (1.0 + preact * (1.0 - logistic))
        cot[:, start : start + TILE] = value.astype(BF16)

    group = iota((CH, CH), 0) // CI
    lane = iota((CH, CH), 1)
    spare = lane - CI * ((group + TAPS) % 8)
    energy = jnp.full((CH, CH), energy_ref[0], F32)
    high, middle, low = (part.astype(F32) for part in parts_of(energy))
    total = jnp.where(spare == 0, high, jnp.where(spare == 1, middle, jnp.where(spare == 2, low, 0.0)))
    for k, (which, shift) in enumerate(SOURCES):
        patch = held[which][pl.ds(SIDE + shift * SIDE, SITES), :]
        block = jnp.dot(cot[...], patch, preferred_element_type=F32)
        block = jnp.where(same, block, 0.0)
        if k:
            block = pltpu.roll(block, k * CI, 1)
        total = total + block
    rows_ref[...] = total.astype(BF16).reshape(G, G, CH)


def update_kernel(
    words_hbm, sector_hbm, energy_hbm, shift_hbm, w_hbm, bias_hbm, readout_hbm, feat_hbm,
    out_ref,
    words_ref, sector_ref, energy_ref, shift_ref, w_ref, bias_ref, readout_ref,
    f0, fp, fm, wb, cot, word_row, rows_ref,
    recv1, send2, recv2, part, sums, wide, gram_ref, cent_ref, work, copy_sems, send_sems, recv_sems,
):
    feature_copies = (
        pltpu.make_async_copy(feat_hbm, f0.at[pl.ds(SIDE, SITES)], copy_sems.at[0]),
        pltpu.make_async_copy(feat_hbm.at[pl.ds(SITES - SIDE, SIDE)], f0.at[pl.ds(0, SIDE)], copy_sems.at[1]),
        pltpu.make_async_copy(feat_hbm.at[pl.ds(0, SIDE)], f0.at[pl.ds(SIDE + SITES, SIDE)], copy_sems.at[2]),
    )
    pairs = (
        (w_hbm, w_ref), (words_hbm, words_ref), (bias_hbm, bias_ref),
        (readout_hbm, readout_ref), (sector_hbm, sector_ref), (energy_hbm, energy_ref), (shift_hbm, shift_ref),
    )
    small_copies = [pltpu.make_async_copy(a, b, copy_sems.at[3 + n]) for n, (a, b) in enumerate(pairs)]
    for copy in small_copies:
        copy.start()
    for copy in feature_copies:
        copy.start()

    samp = lax.axis_index("samp")
    tile = lax.axis_index("tile")
    h = samp // 4
    l = (samp - h * 4) * 4 + tile
    l_samp = samp - h * 4

    def peer_h(other):
        return (other * 4 + l_samp, tile)

    def peer_l(other):
        other_samp = other // 4
        return (h * 4 + other_samp, other - other_samp * 4)

    barrier = pltpu.get_barrier_semaphore()
    for step in range(1, G):
        pl.semaphore_signal(
            barrier, inc=1, device_id=peer_h(lax.rem(h + step, G)), device_id_type=pl.DeviceIdType.MESH
        )
        pl.semaphore_signal(
            barrier, inc=1, device_id=peer_l(lax.rem(l + step, G)), device_id_type=pl.DeviceIdType.MESH
        )

    for copy in small_copies:
        copy.wait()
    local_rows(
        words_ref, sector_ref, energy_ref, w_ref, bias_ref, readout_ref, feature_copies,
        rows_ref, f0, fp, fm, wb, cot, word_row,
    )
    pl.semaphore_wait(barrier, 2 * (G - 1))

    def exchange(stage, mine, peer, source, target):
        def send(step, carry):
            other = lax.rem(mine + step, G)
            pltpu.make_async_remote_copy(
                src_ref=source(other),
                dst_ref=target.at[mine],
                send_sem=send_sems.at[stage],
                recv_sem=recv_sems.at[stage],
                device_id=peer(other),
                device_id_type=pl.DeviceIdType.MESH,
            ).start()
            return carry

        lax.fori_loop(1, G, send, 0)

    def finish(stage, target):
        many = target.at[pl.ds(0, G - 1)]
        pltpu.make_async_copy(many, many, recv_sems.at[stage]).wait()
        pltpu.make_async_copy(many, many, send_sems.at[stage]).wait()

    exchange(0, h, peer_h, lambda other: rows_ref.at[other], recv1)
    recv1[h] = rows_ref[h]
    finish(0, recv1)
    turned_row = iota((NS, NS), 0)
    source_row = (turned_row % G) * G + turned_row // G
    turn = (iota((NS, NS), 1) == source_row).astype(F32).astype(BF16)
    turned = jnp.dot(turn, recv1[...].reshape(NS, CH), preferred_element_type=F32)
    send2[...] = turned.astype(BF16).reshape(G, G, CH)
    exchange(1, l, peer_l, lambda other: send2.at[other], recv2)
    recv2[l] = send2[l]
    finish(1, recv2)

    group = samp // 8
    lane = iota((CH, CH), 1)
    order = (iota((CH, CH), 0) == (lane + group * CI) % CH).astype(F32).astype(BF16)
    raw = jnp.dot(recv2[...].reshape(NS, CH), order, preferred_element_type=F32)
    mean = jnp.mean(raw, axis=0, keepdims=True)
    centered = jnp.where(lane < TAPS * CI, (raw - mean) * (1.0 / math.sqrt(NS)), 0.0)
    energy = jnp.sum(jnp.where(lane >= TAPS * CI, raw, 0.0), axis=1, keepdims=True)
    cent_ref[...] = jnp.where(lane == TAPS * CI, energy, centered)
    partial_gram = lax.dot_general(
        centered, centered, (((1,), (1,)), ((), ())), precision=HIGHEST, preferred_element_type=F32
    )
    part[...] = partial_gram.reshape(G, G, NS)

    exchange(2, l, peer_l, lambda other: part.at[other], sums)
    sums[l] = part[l]
    finish(2, sums)
    wide[h] = jnp.sum(sums[...], axis=0)
    exchange(3, h, peer_h, lambda other: wide.at[h], wide)
    finish(3, wide)
    gram_ref[l] = jnp.sum(wide[...], axis=0)
    exchange(4, l, peer_l, lambda other: gram_ref.at[l], gram_ref)
    finish(4, gram_ref)
    finish_update(shift_ref, gram_ref, cent_ref, out_ref, work)


def update_of(features, spin_words, conv_weight, spin_bias, readout, sector, diag_shift, energy_dev):
    vmem = pl.BlockSpec(memory_space=pltpu.VMEM)
    hbm = pl.BlockSpec(memory_space=pltpu.HBM)
    small = pl.BlockSpec(memory_space=pl.ANY)
    return pl.pallas_call(
        update_kernel,
        out_shape=jax.ShapeDtypeStruct((1, TAPS * CI), F32),
        in_specs=[hbm, small, small, small, hbm, hbm, hbm, hbm],
        out_specs=vmem,
        scratch_shapes=[
            pltpu.VMEM((1, 77), jnp.int32),
            pltpu.SMEM((1,), jnp.int32),
            pltpu.SMEM((1,), F32),
            pltpu.SMEM((1,), F32),
            pltpu.VMEM((TAPS * CI, CH), BF16),
            pltpu.VMEM((1, CH), F32),
            pltpu.VMEM((1, CH), F32),
            pltpu.VMEM((PAD, CH), BF16),
            pltpu.VMEM((PAD, CH), BF16),
            pltpu.VMEM((PAD, CH), BF16),
            pltpu.VMEM((TAPS, CH, CH), BF16),
            pltpu.VMEM((CH, SITES), BF16),
            pltpu.VMEM((1, 128), jnp.int32),
            pltpu.VMEM((G, G, CH), BF16),
            pltpu.VMEM((G, G, CH), BF16),
            pltpu.VMEM((G, G, CH), BF16),
            pltpu.VMEM((G, G, CH), BF16),
            pltpu.VMEM((G, G, NS), F32),
            pltpu.VMEM((G, G, NS), F32),
            pltpu.VMEM((G, G, NS), F32),
            pltpu.VMEM((G, G, NS), F32),
            pltpu.VMEM((NS, CH), F32),
            pltpu.VMEM((NS, NS + 128), F32),
            pltpu.SemaphoreType.DMA((10,)),
            pltpu.SemaphoreType.DMA((5,)),
            pltpu.SemaphoreType.DMA((5,)),
        ],
        compiler_params=pltpu.CompilerParams(
            collective_id=0, has_side_effects=True, vmem_limit_bytes=62 << 20
        ),
        name="update_of",
    )(
        spin_words, sector, energy_dev, diag_shift, conv_weight.T,
        spin_bias.reshape(1, CH), readout.reshape(1, CH), features.reshape(SITES, CH),
    )


def on_device(
    features, spin_words, conv_weight, spin_bias, readout, sector, diag_shift, energy_dev
):
    return update_of(
        features, spin_words, conv_weight, spin_bias, readout, sector, diag_shift, energy_dev
    )


def solution(mesh):
    placed = (
        P(("samp", "tile"), None, None, None),
        P(("samp", "tile"), None),
        P(),
        P(),
        P(),
        P(),
        P(),
        P(("samp", "tile")),
    )
    return jax.shard_map(
        on_device, mesh=mesh, in_specs=placed, out_specs=P(("samp", "tile"), None), check_vma=False
    )
```

```python
import functools
import math

import jax
import jax.numpy as jnp
from jax import lax
from jax.experimental import pallas as pl
from jax.experimental.pallas import tpu as pltpu
from jax.sharding import PartitionSpec as P

SIDE = 48
SITES = SIDE * SIDE
PAD = SITES + 2 * SIDE
CH = 256
CI = 32
TAPS = 7
PARAMS = CH * TAPS * CI
NS = 256
G = 16
SPAN = 2
HALF = NS // 2

SOURCES = ((0, 0), (0, 1), (0, -1), (1, 0), (2, 0), (2, 1), (1, -1))
TILE = 256
F32 = jnp.float32
BF16 = jnp.bfloat16
HIGHEST = lax.Precision.HIGHEST


def iota(shape, dim):
    return lax.broadcasted_iota(jnp.int32, shape, dim)


def column_of(row):
    shape = (CH, CH)
    picked = jnp.where(iota(shape, 0) == iota(shape, 1), jnp.broadcast_to(row, shape), 0.0)
    return jnp.sum(picked, axis=1, keepdims=True)


def parts_of(value):
    high = value.astype(BF16)
    rest = value - high.astype(F32)
    middle = rest.astype(BF16)
    low = (rest - middle.astype(F32)).astype(BF16)
    return high, middle, low


def row_spread(block, j):
    return jnp.broadcast_to(block[j : j + 1, :], (8, 128))


def lane_spread(block, j):
    return jnp.broadcast_to(block[:, j : j + 1], (8, 128))


def total_of(terms):
    while len(terms) > 1:
        odd = terms[-1:] if len(terms) % 2 else []
        terms = [a + b for a, b in zip(terms[::2], terms[1::2])] + odd
    return terms[0]


def eliminate_panel(panel, base):
    sub = iota((8, 128), 0)
    width = len(panel[0])
    for s in range(0, 4, SPAN):
        mine = range(s, s + SPAN)
        own = [list(panel[a]) for a in mine]
        count = 8 * SPAN
        cols = [[lane_spread(rows[0], base + 8 * s + c) for rows in own] for c in range(count)]
        for j in range(count):
            group, line = divmod(j, 8)
            inverse = 1.0 / row_spread(cols[j][group], line)
            here = sub == line
            pivot_row = [row_spread(own[group][t], line) * inverse for t in range(width)]
            pivot_col = {c: row_spread(cols[c][group], line) * inverse for c in range(j + 1, count)}
            for a in range(SPAN):
                factor = cols[j][a]
                for t in range(width):
                    changed = own[a][t] - factor * pivot_row[t]
                    own[a][t] = jnp.where(here, pivot_row[t], changed) if a == group else changed
                for c in range(j + 1, count):
                    changed = cols[c][a] - factor * pivot_col[c]
                    cols[c][a] = jnp.where(here, pivot_col[c], changed) if a == group else changed
        for a, rows in zip(mine, own):
            panel[a] = rows
        spread = [[row_spread(own[c // 8][t], c % 8) for c in range(count)] for t in range(width)]
        for a in range(4):
            if a in mine:
                continue
            factors = [lane_spread(panel[a][0], base + 8 * s + c) for c in range(count)]
            panel[a] = [
                panel[a][t] - total_of([factors[c] * spread[t][c] for c in range(count)]) for t in range(width)
            ]
    return panel


def eliminate(work):
    for q in range(NS // 32):
        half, base = q // 4, 32 * (q % 4)
        lanes = [slice(t * 128, (t + 1) * 128) for t in range(half, 3)]
        rows = [slice(q * 32 + 8 * a, q * 32 + 8 * a + 8) for a in range(4)]
        panel = eliminate_panel([[work[r, at] for at in lanes] for r in rows], base)
        for r, group in zip(rows, panel):
            for at, block in zip(lanes, group):
                work[r, at] = block
        solved = jnp.concatenate([jnp.concatenate(group, axis=1) for group in panel], axis=0)
        mh, mm, ml = (part.astype(F32) for part in parts_of(solved))
        zero = jnp.zeros_like(mh)
        right = jnp.concatenate([mh, mh, mh, mm, ml, mm, zero, zero], axis=0).astype(BF16)
        others = [n for n in range(NS // 32) if n != q]
        for some in ([n for n in others if n == q + 1], [n for n in others if n != q + 1]):
            if some:
                subtract_panel(work, some, lanes, base, right)


def subtract_panel(work, some, lanes, base, right):
    factor = jnp.concatenate([work[n * 32 : n * 32 + 32, lanes[0]] for n in some], axis=0)
    column = iota(factor.shape, 1)
    factor = jnp.where((column >= base) & (column < base + 32), factor, 0.0)
    factor = pltpu.roll(factor, (128 - base) % 128, 1) if base else factor
    fh, fm, fl = (part.astype(F32) for part in parts_of(factor))
    pair = fh + pltpu.roll(fm, 32, 1)
    left = pair + pltpu.roll(fl, 64, 1) + pltpu.roll(fh, 96, 1)
    left = jnp.concatenate([left.astype(BF16), pair.astype(BF16)], axis=1)
    change = jnp.dot(left, right, preferred_element_type=F32)
    for m, n in enumerate(some):
        for t, at in enumerate(lanes):
            part = change[m * 32 : m * 32 + 32, t * 128 : (t + 1) * 128]
            work[n * 32 : n * 32 + 32, at] = work[n * 32 : n * 32 + 32, at] - part


def finish_update(shift_ref, gram_ref, cent_ref, out_ref, work):
    row = iota((HALF, HALF), 0)
    col = iota((HALF, HALF), 1)
    low = slice(0, HALF)
    high = slice(HALF, NS)
    first, second, cross = (gram_ref[:, 8 * n : 8 * n + 8, :].reshape(HALF, HALF) for n in range(3))
    diagonal = jnp.where(row == col, first + second, 0.0)
    trace = jnp.sum(jnp.sum(diagonal, axis=0, keepdims=True), axis=1, keepdims=True)
    shift = shift_ref[0] * (trace * (1.0 / NS))
    work[low, low] = jnp.where(row == col, first + shift, first)
    work[high, high] = jnp.where(row == col, second + shift, second)
    work[high, low] = cross
    work[low, high] = cross.T
    energy_lane = TAPS * CI - 128
    last = cent_ref[:, 128:256]
    work[:, NS : NS + 128] = jnp.where(iota((NS, 128), 1) == energy_lane, last, 0.0)
    eliminate(work)
    answer = work[:, NS + energy_lane : NS + energy_lane + 1]
    raw_step = jnp.sum(answer * cent_ref[...], axis=0, keepdims=True)
    square_sum = jnp.zeros((1, 1), F32)
    weighted = (
        answer[low] * first + 2.0 * answer[high] * cross,
        answer[high] * second,
    )
    for side, product in zip((low, high), weighted):
        flat = jnp.sum(jnp.where(row == col, jnp.broadcast_to(answer[side], (HALF, HALF)), 0.0), axis=0, keepdims=True)
        square_sum += jnp.sum(jnp.sum(product, axis=0, keepdims=True) * flat, axis=1, keepdims=True)
    update = -raw_step / jnp.sqrt(square_sum / PARAMS + 1e-06)
    out_ref[...] = update[:, 0 : TAPS * CI]


def local_rows(
    words_ref, sector_ref, energy_ref, w_ref, bias_ref, readout_ref, feature_copies,
    rows_ref, f0, fp, fm, wb, cot, word_row,
):
    weight = w_ref[...]
    same = (iota((CH, CH), 0) // CI) == (iota((CH, CH), 1) // CI)
    source_row = iota((TAPS * CI, CH), 0)
    lane_in = iota((TAPS * CI, CH), 1) % CI
    for k in range(TAPS):
        spread = (source_row == lane_in + k * CI).astype(F32).astype(BF16)
        block = lax.dot_general(weight, spread, (((0,), (0,)), ((), ())), preferred_element_type=F32)
        wb[k] = jnp.where(same, block, 0.0).astype(BF16)

    word_row[...] = jnp.zeros_like(word_row)
    word_row[:, 0:77] = words_ref[...]
    bits = (jnp.broadcast_to(word_row[...], (32, 128)) >> iota((32, 128), 0)) & 1
    bits = bits.astype(F32).astype(BF16)
    site = iota((1, SITES), 1)
    word_of = site // 30
    bit_of = site - 30 * word_of
    pick_word = (iota((128, SITES), 0) == jnp.broadcast_to(word_of, (128, SITES))).astype(F32).astype(BF16)
    spread_bits = jnp.dot(bits, pick_word, preferred_element_type=F32)
    pick_bit = iota((32, SITES), 0) == jnp.broadcast_to(bit_of, (32, SITES))
    sign = 2.0 * jnp.sum(jnp.where(pick_bit, spread_bits, 0.0), axis=0, keepdims=True) - 1.0

    sector = sector_ref[0]
    wave_row = sector // SIDE
    wave_col = sector - wave_row * SIDE
    site_i = site // SIDE
    site_j = site - SIDE * site_i
    wave_arg = (wave_row * site_i + wave_col * site_j) % SIDE
    phase = jnp.cos(2.0 * math.pi / SIDE * wave_arg.astype(F32))

    bias = column_of(bias_ref[...])
    readout = column_of(readout_ref[...])

    for copy in feature_copies:
        copy.wait()
    for row in range(SIDE + 2):
        rows = pl.ds(row * SIDE, SIDE)
        wide = f0[rows, :].astype(F32)
        fp[rows, :] = pltpu.roll(wide, SIDE - 1, 0).astype(BF16)
        fm[rows, :] = pltpu.roll(wide, 1, 0).astype(BF16)

    held = (f0, fp, fm)
    for t in range(SITES // TILE):
        start = t * TILE
        preact = bias * sign[:, start : start + TILE]
        for k, (which, shift) in enumerate(SOURCES):
            patch = held[which][pl.ds(SIDE + start + shift * SIDE, TILE), :]
            preact = preact + lax.dot_general(
                wb[k], patch, (((1,), (1,)), ((), ())), preferred_element_type=F32
            )
        logistic = 0.5 + 0.5 * jnp.tanh(0.5 * preact)
        scale = readout * phase[:, start : start + TILE]
        value = scale * logistic * (1.0 + preact * (1.0 - logistic))
        cot[:, start : start + TILE] = value.astype(BF16)

    group = iota((CH, CH), 0) // CI
    lane = iota((CH, CH), 1)
    spare = lane - CI * ((group + TAPS) % 8)
    energy = jnp.full((CH, CH), energy_ref[0], F32)
    high, middle, low = (part.astype(F32) for part in parts_of(energy))
    total = jnp.where(spare == 0, high, jnp.where(spare == 1, middle, jnp.where(spare == 2, low, 0.0)))
    for k, (which, shift) in enumerate(SOURCES):
        patch = held[which][pl.ds(SIDE + shift * SIDE, SITES), :]
        block = jnp.dot(cot[...], patch, preferred_element_type=F32)
        block = jnp.where(same, block, 0.0)
        if k:
            block = pltpu.roll(block, k * CI, 1)
        total = total + block
    rows_ref[...] = total.astype(BF16).reshape(G, G, CH)


def farthest_first(distance):
    pairs = [(a, b) for a in range(4) for b in range(4) if a or b]
    return sorted(pairs, key=lambda pair: -distance(*pair))


def update_kernel(
    words_hbm, sector_hbm, energy_hbm, shift_hbm, w_hbm, bias_hbm, readout_hbm, feat_hbm,
    out_ref,
    words_ref, sector_ref, energy_ref, shift_ref, w_ref, bias_ref, readout_ref,
    f0, fp, fm, wb, cot, word_row, rows_ref,
    recv1, send2, recv2, part, sums, wide, gram_ref, cent_ref, work, copy_sems, send_sems, recv_sems,
):
    feature_copies = (
        pltpu.make_async_copy(feat_hbm, f0.at[pl.ds(SIDE, SITES)], copy_sems.at[0]),
        pltpu.make_async_copy(feat_hbm.at[pl.ds(SITES - SIDE, SIDE)], f0.at[pl.ds(0, SIDE)], copy_sems.at[1]),
        pltpu.make_async_copy(feat_hbm.at[pl.ds(0, SIDE)], f0.at[pl.ds(SIDE + SITES, SIDE)], copy_sems.at[2]),
    )
    pairs = (
        (w_hbm, w_ref), (words_hbm, words_ref), (bias_hbm, bias_ref),
        (readout_hbm, readout_ref), (sector_hbm, sector_ref), (energy_hbm, energy_ref), (shift_hbm, shift_ref),
    )
    small_copies = [pltpu.make_async_copy(a, b, copy_sems.at[3 + n]) for n, (a, b) in enumerate(pairs)]
    for copy in small_copies:
        copy.start()
    for copy in feature_copies:
        copy.start()

    samp = lax.axis_index("samp")
    tile = lax.axis_index("tile")
    h = samp // 4
    l = (samp - h * 4) * 4 + tile
    l_samp = samp - h * 4

    def peer_h(other):
        return (other * 4 + l_samp, tile)

    def peer_l(other):
        return (h * 4 + other // 4, lax.rem(other, 4))

    y, z_high, inner = h // 4, lax.rem(h, 4), l // 4
    steps_h = farthest_first(lambda a, b: min(a, 4 - a) + 2 * min(b, 4 - b))
    others_h = [lax.rem(y + a, 4) * 4 + lax.rem(z_high + b, 4) for a, b in steps_h]
    steps_l = farthest_first(lambda a, b: a // 2 + min(b, 4 - b))
    others_l = [lax.bitwise_xor(inner, a) * 4 + lax.rem(tile + b, 4) for a, b in steps_l]

    barrier = pltpu.get_barrier_semaphore()
    for other_h, other_l in zip(others_h, others_l):
        pl.semaphore_signal(barrier, inc=1, device_id=peer_h(other_h), device_id_type=pl.DeviceIdType.MESH)
        pl.semaphore_signal(barrier, inc=1, device_id=peer_l(other_l), device_id_type=pl.DeviceIdType.MESH)

    for copy in small_copies:
        copy.wait()
    local_rows(
        words_ref, sector_ref, energy_ref, w_ref, bias_ref, readout_ref, feature_copies,
        rows_ref, f0, fp, fm, wb, cot, word_row,
    )
    pl.semaphore_wait(barrier, 2 * (G - 1))

    def exchange(stage, mine, others, peer, source, target):
        for other in others:
            pltpu.make_async_remote_copy(
                src_ref=source(other),
                dst_ref=target.at[mine],
                send_sem=send_sems.at[stage],
                recv_sem=recv_sems.at[stage],
                device_id=peer(other),
                device_id_type=pl.DeviceIdType.MESH,
            ).start()

    def arrived(sems, stage, target):
        many = target.at[pl.ds(0, G - 1)]
        pltpu.make_async_copy(many, many, sems.at[stage]).wait()

    exchange(0, h, others_h, peer_h, lambda other: rows_ref.at[other], recv1)
    recv1[h] = rows_ref[h]
    turned_row = iota((NS, NS), 0)
    source_row = (turned_row % G) * G + turned_row // G
    turn = (iota((NS, NS), 1) == source_row).astype(F32).astype(BF16)
    group = samp // 8
    lane = iota((CH, CH), 1)
    order = (iota((CH, CH), 0) == (lane + group * CI) % CH).astype(F32).astype(BF16)
    arrived(recv_sems, 0, recv1)
    turned = jnp.dot(turn, recv1[...].reshape(NS, CH), preferred_element_type=F32)
    send2[...] = turned.astype(BF16).reshape(G, G, CH)
    exchange(1, l, others_l, peer_l, lambda other: send2.at[other], recv2)
    recv2[l] = send2[l]
    arrived(recv_sems, 1, recv2)

    raw = jnp.dot(recv2[...].reshape(NS, CH), order, preferred_element_type=F32)
    mean = jnp.mean(raw, axis=0, keepdims=True)
    centered = jnp.where(lane < TAPS * CI, (raw - mean) * (1.0 / math.sqrt(NS)), 0.0)
    low, high = centered[:HALF], centered[HALF:]
    for n, (left, right) in enumerate(((low, low), (high, high), (high, low))):
        block = lax.dot_general(
            left, right, (((1,), (1,)), ((), ())), precision=HIGHEST, preferred_element_type=F32
        )
        part[:, 8 * n : 8 * n + 8, :] = block.reshape(G, 8, HALF)

    exchange(2, l, others_l, peer_l, lambda other: part.at[other], sums)
    sums[l] = part[l]
    energy = jnp.sum(jnp.where(lane >= TAPS * CI, raw, 0.0), axis=1, keepdims=True)
    cent_ref[...] = jnp.where(lane == TAPS * CI, energy, centered)
    arrived(recv_sems, 2, sums)
    wide[h] = jnp.sum(sums[...], axis=0)
    exchange(3, h, others_h, peer_h, lambda other: wide.at[h], wide)
    arrived(recv_sems, 3, wide)
    gram_ref[l] = jnp.sum(wide[...], axis=0)
    exchange(4, l, others_l, peer_l, lambda other: gram_ref.at[l], gram_ref)
    arrived(recv_sems, 4, gram_ref)
    finish_update(shift_ref, gram_ref, cent_ref, out_ref, work)
    for stage, sent in enumerate((recv1, recv2, sums, wide, gram_ref)):
        arrived(send_sems, stage, sent)


def update_of(features, spin_words, conv_weight, spin_bias, readout, sector, diag_shift, energy_dev):
    vmem = pl.BlockSpec(memory_space=pltpu.VMEM)
    hbm = pl.BlockSpec(memory_space=pltpu.HBM)
    small = pl.BlockSpec(memory_space=pl.ANY)
    return pl.pallas_call(
        update_kernel,
        out_shape=jax.ShapeDtypeStruct((1, TAPS * CI), F32),
        in_specs=[hbm, small, small, small, hbm, hbm, hbm, hbm],
        out_specs=vmem,
        scratch_shapes=[
            pltpu.VMEM((1, 77), jnp.int32),
            pltpu.SMEM((1,), jnp.int32),
            pltpu.SMEM((1,), F32),
            pltpu.SMEM((1,), F32),
            pltpu.VMEM((TAPS * CI, CH), BF16),
            pltpu.VMEM((1, CH), F32),
            pltpu.VMEM((1, CH), F32),
            pltpu.VMEM((PAD, CH), BF16),
            pltpu.VMEM((PAD, CH), BF16),
            pltpu.VMEM((PAD, CH), BF16),
            pltpu.VMEM((TAPS, CH, CH), BF16),
            pltpu.VMEM((CH, SITES), BF16),
            pltpu.VMEM((1, 128), jnp.int32),
            pltpu.VMEM((G, G, CH), BF16),
            pltpu.VMEM((G, G, CH), BF16),
            pltpu.VMEM((G, G, CH), BF16),
            pltpu.VMEM((G, G, CH), BF16),
            pltpu.VMEM((G, 24, HALF), F32),
            pltpu.VMEM((G, 24, HALF), F32),
            pltpu.VMEM((G, 24, HALF), F32),
            pltpu.VMEM((G, 24, HALF), F32),
            pltpu.VMEM((NS, CH), F32),
            pltpu.VMEM((NS, NS + 128), F32),
            pltpu.SemaphoreType.DMA((10,)),
            pltpu.SemaphoreType.DMA((5,)),
            pltpu.SemaphoreType.DMA((5,)),
        ],
        compiler_params=pltpu.CompilerParams(
            collective_id=0, has_side_effects=True, vmem_limit_bytes=62 << 20
        ),
        name="update_of",
    )(
        spin_words, sector, energy_dev, diag_shift, conv_weight.T,
        spin_bias.reshape(1, CH), readout.reshape(1, CH), features.reshape(SITES, CH),
    )


def on_device(
    features, spin_words, conv_weight, spin_bias, readout, sector, diag_shift, energy_dev
):
    return update_of(
        features, spin_words, conv_weight, spin_bias, readout, sector, diag_shift, energy_dev
    )


def solution(mesh):
    placed = (
        P(("samp", "tile"), None, None, None),
        P(("samp", "tile"), None),
        P(),
        P(),
        P(),
        P(),
        P(),
        P(("samp", "tile")),
    )
    return jax.shard_map(
        on_device, mesh=mesh, in_specs=placed, out_specs=P(("samp", "tile"), None), check_vma=False
    )
```

```python
import functools
import math

import jax
import jax.numpy as jnp
from jax import lax
from jax.experimental import pallas as pl
from jax.experimental.pallas import tpu as pltpu
from jax.sharding import PartitionSpec as P

SIDE = 48
SITES = SIDE * SIDE
PAD = SITES + 2 * SIDE
CH = 256
CI = 32
TAPS = 7
PARAMS = CH * TAPS * CI
NS = 256
G = 16
SPAN = 2
HALF = NS // 2

SOURCES = ((0, 0), (0, 1), (0, -1), (1, 0), (2, 0), (2, 1), (1, -1))
TILE = 256
F32 = jnp.float32
BF16 = jnp.bfloat16
HIGHEST = lax.Precision.HIGHEST


def iota(shape, dim):
    return lax.broadcasted_iota(jnp.int32, shape, dim)


def column_of(row):
    shape = (CH, CH)
    picked = jnp.where(iota(shape, 0) == iota(shape, 1), jnp.broadcast_to(row, shape), 0.0)
    return jnp.sum(picked, axis=1, keepdims=True)


def parts_of(value):
    high = value.astype(BF16)
    rest = value - high.astype(F32)
    middle = rest.astype(BF16)
    low = (rest - middle.astype(F32)).astype(BF16)
    return high, middle, low


def row_spread(block, j):
    return jnp.broadcast_to(block[j : j + 1, :], (8, 128))


def lane_spread(block, j):
    return jnp.take_along_axis(block, jnp.full((8, 128), j, jnp.int32), axis=1)


def total_of(terms):
    while len(terms) > 1:
        odd = terms[-1:] if len(terms) % 2 else []
        terms = [a + b for a, b in zip(terms[::2], terms[1::2])] + odd
    return terms[0]


def eliminate_panel(panel, base):
    sub = iota((8, 128), 0)
    width = len(panel[0])
    for s in range(0, 4, SPAN):
        mine = range(s, s + SPAN)
        own = [list(panel[a]) for a in mine]
        count = 8 * SPAN
        cols = [[lane_spread(rows[0], base + 8 * s + c) for rows in own] for c in range(count)]
        inverses = []
        for j in range(0, count, 2):
            group, line = divmod(j, 8)
            corner = row_spread(cols[j][group], line)
            beside = row_spread(cols[j + 1][group], line)
            below = row_spread(cols[j][group], line + 1)
            last = row_spread(cols[j + 1][group], line + 1)
            first_inverse = 1.0 / corner
            ratio = below * first_inverse
            second_inverse = 1.0 / (last - ratio * beside)
            inverses += [first_inverse, second_inverse]
            first = [cols[j][a] * first_inverse for a in range(SPAN)]
            first[group] = jnp.where(sub == line, 0.0, first[group])
            second = [(cols[j + 1][a] - first[a] * beside) * second_inverse for a in range(SPAN)]
            second[group] = jnp.where(sub == line + 1, 0.0, second[group])

            def reduced(blocks):
                upper = row_spread(blocks[group], line)
                lower = row_spread(blocks[group], line + 1) - ratio * upper
                return [(blocks[a] - first[a] * upper) - second[a] * lower for a in range(SPAN)]

            for c in range(j + 2, count):
                cols[c] = reduced(cols[c])
            for t in range(width):
                for a, block in enumerate(reduced([rows[t] for rows in own])):
                    own[a][t] = block
        for a in range(SPAN):
            scale = inverses[8 * a]
            for line in range(1, 8):
                scale = jnp.where(sub == line, inverses[8 * a + line], scale)
            own[a] = [block * scale for block in own[a]]
        for a, rows in zip(mine, own):
            panel[a] = rows
        spread = [[row_spread(own[c // 8][t], c % 8) for c in range(count)] for t in range(width)]
        for a in range(len(panel)):
            if a in mine:
                continue
            factors = [lane_spread(panel[a][0], base + 8 * s + c) for c in range(count)]
            panel[a] = [
                panel[a][t] - total_of([factors[c] * spread[t][c] for c in range(count)]) for t in range(width)
            ]
    return panel


def eliminate(work):
    for q in range(NS // 32):
        half, base = q // 4, 32 * (q % 4)
        lanes = [slice(t * 128, (t + 1) * 128) for t in range(half, 3)]
        near = [2 * q, 2 * q + 1] + [2 * q + 2] * (q + 1 < NS // 32)
        rows = [slice(n * 16 + 8 * a, n * 16 + 8 * a + 8) for n in near for a in range(2)]
        panel = eliminate_panel([[work[r, at] for at in lanes] for r in rows], base)
        for r, group in zip(rows, panel):
            for at, block in zip(lanes, group):
                work[r, at] = block
        solved = jnp.concatenate([jnp.concatenate(group, axis=1) for group in panel[:4]], axis=0)
        mh, mm, ml = (part.astype(F32) for part in parts_of(solved))
        zero = jnp.zeros_like(mh)
        right = jnp.concatenate([mh, mh, mh, mm, ml, mm, zero, zero], axis=0).astype(BF16)
        far = [n % 16 for n in range(2 * q + 3, 2 * q + 19) if n % 16 not in near]
        subtract_panel(work, far, lanes, base, right)


def subtract_panel(work, some, lanes, base, right):
    factor = jnp.concatenate([work[n * 16 : n * 16 + 16, lanes[0]] for n in some], axis=0)
    column = iota(factor.shape, 1)
    factor = jnp.where((column >= base) & (column < base + 32), factor, 0.0)
    factor = pltpu.roll(factor, (128 - base) % 128, 1) if base else factor
    fh, fm, fl = (part.astype(F32) for part in parts_of(factor))
    pair = fh + pltpu.roll(fm, 32, 1)
    left = pair + pltpu.roll(fl, 64, 1) + pltpu.roll(fh, 96, 1)
    left = jnp.concatenate([left.astype(BF16), pair.astype(BF16)], axis=1)
    change = jnp.dot(left, right, preferred_element_type=F32)
    for m, n in enumerate(some):
        for t, at in enumerate(lanes):
            part = change[m * 16 : m * 16 + 16, t * 128 : (t + 1) * 128]
            work[n * 16 : n * 16 + 16, at] = work[n * 16 : n * 16 + 16, at] - part


def finish_update(shift_ref, gram_ref, cent_ref, out_ref, work):
    row = iota((HALF, HALF), 0)
    col = iota((HALF, HALF), 1)
    low = slice(0, HALF)
    high = slice(HALF, NS)
    first, second, cross = (gram_ref[:, 8 * n : 8 * n + 8, :].reshape(HALF, HALF) for n in range(3))
    diagonal = jnp.where(row == col, first + second, 0.0)
    trace = jnp.sum(jnp.sum(diagonal, axis=0, keepdims=True), axis=1, keepdims=True)
    shift = shift_ref[0] * (trace * (1.0 / NS))
    work[low, low] = jnp.where(row == col, first + shift, first)
    work[high, high] = jnp.where(row == col, second + shift, second)
    work[high, low] = cross
    work[low, high] = cross.T
    energy_lane = TAPS * CI - 128
    last = cent_ref[:, 128:256]
    work[:, NS : NS + 128] = jnp.where(iota((NS, 128), 1) == energy_lane, last, 0.0)
    eliminate(work)
    answer = work[:, NS + energy_lane : NS + energy_lane + 1]
    raw_step = jnp.sum(answer * cent_ref[...], axis=0, keepdims=True)
    square_sum = jnp.zeros((1, 1), F32)
    weighted = (
        answer[low] * first + 2.0 * answer[high] * cross,
        answer[high] * second,
    )
    for side, product in zip((low, high), weighted):
        flat = jnp.sum(jnp.where(row == col, jnp.broadcast_to(answer[side], (HALF, HALF)), 0.0), axis=0, keepdims=True)
        square_sum += jnp.sum(jnp.sum(product, axis=0, keepdims=True) * flat, axis=1, keepdims=True)
    update = -raw_step / jnp.sqrt(square_sum / PARAMS + 1e-06)
    out_ref[...] = update[:, 0 : TAPS * CI]


def local_rows(
    words_ref, sector_ref, energy_ref, w_ref, bias_ref, readout_ref, feature_copies,
    rows_ref, f0, fp, fm, wb, cot, word_row,
):
    weight = w_ref[...]
    source_row = iota((TAPS * CI, CH), 0)
    lane_in = iota((TAPS * CI, CH), 1)
    same = iota((CH, CH), 0) // CI % 4 == iota((CH, CH), 1) // CI % 4
    for pair in range(4):
        wanted = lane_in % CI + (2 * pair + lane_in // HALF) * CI
        spread = (source_row == wanted).astype(F32).astype(BF16)
        block = lax.dot_general(weight, spread, (((0,), (0,)), ((), ())), preferred_element_type=F32)
        wb[pair] = jnp.where(same, block, 0.0).astype(BF16)

    word_row[...] = jnp.zeros_like(word_row)
    word_row[:, 0:77] = words_ref[...]
    bits = (jnp.broadcast_to(word_row[...], (32, 128)) >> iota((32, 128), 0)) & 1
    bits = bits.astype(F32).astype(BF16)
    site = iota((1, SITES), 1)
    word_of = site // 30
    bit_of = site - 30 * word_of
    pick_word = (iota((128, SITES), 0) == jnp.broadcast_to(word_of, (128, SITES))).astype(F32).astype(BF16)
    spread_bits = jnp.dot(bits, pick_word, preferred_element_type=F32)
    pick_bit = iota((32, SITES), 0) == jnp.broadcast_to(bit_of, (32, SITES))
    sign = 2.0 * jnp.sum(jnp.where(pick_bit, spread_bits, 0.0), axis=0, keepdims=True) - 1.0

    sector = sector_ref[0]
    wave_row = sector // SIDE
    wave_col = sector - wave_row * SIDE
    site_i = site // SIDE
    site_j = site - SIDE * site_i
    wave_arg = (wave_row * site_i + wave_col * site_j) % SIDE
    phase = jnp.cos(2.0 * math.pi / SIDE * wave_arg.astype(F32))

    bias = column_of(bias_ref[...])
    readout = column_of(readout_ref[...])

    for copy in feature_copies:
        copy.wait()
    for row in range(SIDE + 2):
        rows = pl.ds(row * SIDE, SIDE)
        wide = f0[rows, :].astype(F32)
        fp[rows, :] = pltpu.roll(wide, SIDE - 1, 0).astype(BF16)
        fm[rows, :] = pltpu.roll(wide, 1, 0).astype(BF16)

    held = (f0, fp, fm)
    for t in range(SITES // TILE):
        start = t * TILE
        preact = [bias[:HALF] * sign[:, start : start + TILE], bias[HALF:] * sign[:, start : start + TILE]]
        for n in range(2):
            half = slice(n * HALF, n * HALF + HALF)
            for pair, taps in enumerate(((0, 1), (2, 3), (4, 5), (6,))):
                patch = jnp.concatenate(
                    [
                        held[which][pl.ds(SIDE + start + shift * SIDE, TILE), half]
                        for which, shift in (SOURCES[k] for k in taps)
                    ],
                    axis=1,
                )
                weight = wb[pair, half, 0 : HALF * len(taps)]
                preact[n] += lax.dot_general(
                    weight, patch, (((1,), (1,)), ((), ())), preferred_element_type=F32
                )
        preact = jnp.concatenate(preact, axis=0)
        logistic = 0.5 + 0.5 * jnp.tanh(0.5 * preact)
        scale = readout * phase[:, start : start + TILE]
        value = scale * logistic * (1.0 + preact * (1.0 - logistic))
        cot[:, start : start + TILE] = value.astype(BF16)

    group = iota((HALF, HALF), 0) // CI
    lane = iota((HALF, HALF), 1)
    same_half = group == lane // CI
    spare = lane - CI * ((group + TAPS) % 4)
    energy = jnp.full((HALF, HALF), energy_ref[0], F32)
    high, middle, low = (part.astype(F32) for part in parts_of(energy))
    spare = jnp.where(spare == 0, high, jnp.where(spare == 1, middle, jnp.where(spare == 2, low, 0.0)))
    for n in range(2):
        half = slice(n * HALF, n * HALF + HALF)
        tiles = [jnp.zeros((HALF, HALF), F32), spare]
        for taps in ((0, 1), (2, 3), (4, 5), (6,)):
            patch = jnp.concatenate(
                [held[which][pl.ds(SIDE + shift * SIDE, SITES), half] for which, shift in (SOURCES[k] for k in taps)],
                axis=1,
            )
            block = jnp.dot(cot[half, :], patch, preferred_element_type=F32)
            for m, k in enumerate(taps):
                piece = jnp.where(same_half, block[:, m * HALF : m * HALF + HALF], 0.0)
                tiles[k // 4] += pltpu.roll(piece, (k % 4) * CI, 1) if k % 4 else piece
        rows_ref[n * 8 : n * 8 + 8] = jnp.concatenate(tiles, axis=1).astype(BF16).reshape(8, G, CH)


def farthest_first(distance):
    pairs = [(a, b) for a in range(4) for b in range(4) if a or b]
    return sorted(pairs, key=lambda pair: -distance(*pair))


def update_kernel(
    words_hbm, sector_hbm, energy_hbm, shift_hbm, w_hbm, bias_hbm, readout_hbm, feat_hbm,
    out_ref,
    words_ref, sector_ref, energy_ref, shift_ref, w_ref, bias_ref, readout_ref,
    f0, fp, fm, wb, cot, word_row, rows_ref,
    recv1, send2, recv2, part, sums, wide, gram_ref, cent_ref, work, copy_sems, send_sems, recv_sems,
):
    feature_copies = (
        pltpu.make_async_copy(feat_hbm, f0.at[pl.ds(SIDE, SITES)], copy_sems.at[0]),
        pltpu.make_async_copy(feat_hbm.at[pl.ds(SITES - SIDE, SIDE)], f0.at[pl.ds(0, SIDE)], copy_sems.at[1]),
        pltpu.make_async_copy(feat_hbm.at[pl.ds(0, SIDE)], f0.at[pl.ds(SIDE + SITES, SIDE)], copy_sems.at[2]),
    )
    pairs = (
        (w_hbm, w_ref), (words_hbm, words_ref), (bias_hbm, bias_ref),
        (readout_hbm, readout_ref), (sector_hbm, sector_ref), (energy_hbm, energy_ref), (shift_hbm, shift_ref),
    )
    small_copies = [pltpu.make_async_copy(a, b, copy_sems.at[3 + n]) for n, (a, b) in enumerate(pairs)]
    for copy in small_copies:
        copy.start()
    for copy in feature_copies:
        copy.start()

    samp = lax.axis_index("samp")
    tile = lax.axis_index("tile")
    h = samp // 4
    l = (samp - h * 4) * 4 + tile
    l_samp = samp - h * 4

    def peer_h(other):
        return (other * 4 + l_samp, tile)

    def peer_l(other):
        return (h * 4 + other // 4, lax.rem(other, 4))

    y, z_high, inner = h // 4, lax.rem(h, 4), l // 4
    steps_h = farthest_first(lambda a, b: min(a, 4 - a) + 2 * min(b, 4 - b))
    others_h = [lax.rem(y + a, 4) * 4 + lax.rem(z_high + b, 4) for a, b in steps_h]
    steps_l = farthest_first(lambda a, b: a // 2 + min(b, 4 - b))
    others_l = [lax.bitwise_xor(inner, a) * 4 + lax.rem(tile + b, 4) for a, b in steps_l]

    barrier = pltpu.get_barrier_semaphore()
    for other_h, other_l in zip(others_h, others_l):
        pl.semaphore_signal(barrier, inc=1, device_id=peer_h(other_h), device_id_type=pl.DeviceIdType.MESH)
        pl.semaphore_signal(barrier, inc=1, device_id=peer_l(other_l), device_id_type=pl.DeviceIdType.MESH)

    for copy in small_copies:
        copy.wait()
    local_rows(
        words_ref, sector_ref, energy_ref, w_ref, bias_ref, readout_ref, feature_copies,
        rows_ref, f0, fp, fm, wb, cot, word_row,
    )
    pl.semaphore_wait(barrier, 2 * (G - 1))

    def exchange(stage, mine, others, peer, source, target):
        for other in others:
            pltpu.make_async_remote_copy(
                src_ref=source(other),
                dst_ref=target.at[mine],
                send_sem=send_sems.at[stage],
                recv_sem=recv_sems.at[stage],
                device_id=peer(other),
                device_id_type=pl.DeviceIdType.MESH,
            ).start()

    def arrived(sems, stage, target):
        many = target.at[pl.ds(0, G - 1)]
        pltpu.make_async_copy(many, many, sems.at[stage]).wait()

    exchange(0, h, others_h, peer_h, lambda other: rows_ref.at[other], recv1)
    recv1[h] = rows_ref[h]
    turned_row = iota((NS, NS), 0)
    source_row = (turned_row % G) * G + turned_row // G
    turn = (iota((NS, NS), 1) == source_row).astype(F32).astype(BF16)
    group = samp // 8
    lane = iota((CH, CH), 1)
    moved = lane // HALF * HALF + (lane % HALF + group * CI) % HALF
    order = (iota((CH, CH), 0) == moved).astype(F32).astype(BF16)
    arrived(recv_sems, 0, recv1)
    turned = jnp.dot(turn, recv1[...].reshape(NS, CH), preferred_element_type=F32)
    send2[...] = turned.astype(BF16).reshape(G, G, CH)
    exchange(1, l, others_l, peer_l, lambda other: send2.at[other], recv2)
    recv2[l] = send2[l]
    arrived(recv_sems, 1, recv2)

    raw = jnp.dot(recv2[...].reshape(NS, CH), order, preferred_element_type=F32)
    mean = jnp.mean(raw, axis=0, keepdims=True)
    centered = jnp.where(lane < TAPS * CI, (raw - mean) * (1.0 / math.sqrt(NS)), 0.0)
    low, high = centered[:HALF], centered[HALF:]
    for n, (left, right) in enumerate(((low, low), (high, high), (high, low))):
        block = lax.dot_general(
            left, right, (((1,), (1,)), ((), ())), precision=HIGHEST, preferred_element_type=F32
        )
        part[:, 8 * n : 8 * n + 8, :] = block.reshape(G, 8, HALF)

    exchange(2, l, others_l, peer_l, lambda other: part.at[other], sums)
    sums[l] = part[l]
    energy = jnp.sum(jnp.where(lane >= TAPS * CI, raw, 0.0), axis=1, keepdims=True)
    cent_ref[...] = jnp.where(lane == TAPS * CI, energy, centered)
    arrived(recv_sems, 2, sums)
    wide[h] = jnp.sum(sums[...], axis=0)
    exchange(3, h, others_h, peer_h, lambda other: wide.at[h], wide)
    arrived(recv_sems, 3, wide)
    gram_ref[l] = jnp.sum(wide[...], axis=0)
    exchange(4, l, others_l, peer_l, lambda other: gram_ref.at[l], gram_ref)
    arrived(recv_sems, 4, gram_ref)
    finish_update(shift_ref, gram_ref, cent_ref, out_ref, work)
    for stage, sent in enumerate((recv1, recv2, sums, wide, gram_ref)):
        arrived(send_sems, stage, sent)


def update_of(features, spin_words, conv_weight, spin_bias, readout, sector, diag_shift, energy_dev):
    vmem = pl.BlockSpec(memory_space=pltpu.VMEM)
    hbm = pl.BlockSpec(memory_space=pltpu.HBM)
    small = pl.BlockSpec(memory_space=pl.ANY)
    return pl.pallas_call(
        update_kernel,
        out_shape=jax.ShapeDtypeStruct((1, TAPS * CI), F32),
        in_specs=[hbm, small, small, small, hbm, hbm, hbm, hbm],
        out_specs=vmem,
        scratch_shapes=[
            pltpu.VMEM((1, 77), jnp.int32),
            pltpu.SMEM((1,), jnp.int32),
            pltpu.SMEM((1,), F32),
            pltpu.SMEM((1,), F32),
            pltpu.VMEM((TAPS * CI, CH), BF16),
            pltpu.VMEM((1, CH), F32),
            pltpu.VMEM((1, CH), F32),
            pltpu.VMEM((PAD, CH), BF16),
            pltpu.VMEM((PAD, CH), BF16),
            pltpu.VMEM((PAD, CH), BF16),
            pltpu.VMEM((4, CH, CH), BF16),
            pltpu.VMEM((CH, SITES), BF16),
            pltpu.VMEM((1, 128), jnp.int32),
            pltpu.VMEM((G, G, CH), BF16),
            pltpu.VMEM((G, G, CH), BF16),
            pltpu.VMEM((G, G, CH), BF16),
            pltpu.VMEM((G, G, CH), BF16),
            pltpu.VMEM((G, 24, HALF), F32),
            pltpu.VMEM((G, 24, HALF), F32),
            pltpu.VMEM((G, 24, HALF), F32),
            pltpu.VMEM((G, 24, HALF), F32),
            pltpu.VMEM((NS, CH), F32),
            pltpu.VMEM((NS, NS + 128), F32),
            pltpu.SemaphoreType.DMA((10,)),
            pltpu.SemaphoreType.DMA((5,)),
            pltpu.SemaphoreType.DMA((5,)),
        ],
        compiler_params=pltpu.CompilerParams(
            collective_id=0, has_side_effects=True, vmem_limit_bytes=62 << 20
        ),
        name="update_of",
    )(
        spin_words, sector, energy_dev, diag_shift, conv_weight.T,
        spin_bias.reshape(1, CH), readout.reshape(1, CH), features.reshape(SITES, CH),
    )


def on_device(
    features, spin_words, conv_weight, spin_bias, readout, sector, diag_shift, energy_dev
):
    return update_of(
        features, spin_words, conv_weight, spin_bias, readout, sector, diag_shift, energy_dev
    )


def solution(mesh):
    placed = (
        P(("samp", "tile"), None, None, None),
        P(("samp", "tile"), None),
        P(),
        P(),
        P(),
        P(),
        P(),
        P(("samp", "tile")),
    )
    return jax.shard_map(
        on_device, mesh=mesh, in_specs=placed, out_specs=P(("samp", "tile"), None), check_vma=False
    )
```

```python
import functools
import math

import jax
import jax.numpy as jnp
from jax import lax
from jax.experimental import pallas as pl
from jax.experimental.pallas import tpu as pltpu
from jax.sharding import PartitionSpec as P

SIDE = 48
SITES = SIDE * SIDE
PAD = SITES + 2 * SIDE
CH = 256
CI = 32
TAPS = 7
PARAMS = CH * TAPS * CI
NS = 256
G = 16
SPAN = 2
HALF = NS // 2

SOURCES = ((0, 0), (0, 1), (0, -1), (1, 0), (2, 0), (2, 1), (1, -1))
TILE = 256
F32 = jnp.float32
BF16 = jnp.bfloat16
HIGHEST = lax.Precision.HIGHEST


def iota(shape, dim):
    return lax.broadcasted_iota(jnp.int32, shape, dim)


def column_of(row):
    shape = (CH, CH)
    picked = jnp.where(iota(shape, 0) == iota(shape, 1), jnp.broadcast_to(row, shape), 0.0)
    return jnp.sum(picked, axis=1, keepdims=True)


def parts_of(value):
    high = value.astype(BF16)
    rest = value - high.astype(F32)
    middle = rest.astype(BF16)
    low = (rest - middle.astype(F32)).astype(BF16)
    return high, middle, low


def row_spread(block, j):
    return jnp.broadcast_to(block[j : j + 1, :], (8, 128))


def lane_spread(block, j):
    return jnp.take_along_axis(block, jnp.full((8, 128), j, jnp.int32), axis=1)


def total_of(terms):
    while len(terms) > 1:
        odd = terms[-1:] if len(terms) % 2 else []
        terms = [a + b for a, b in zip(terms[::2], terms[1::2])] + odd
    return terms[0]


def eliminate_panel(panel, base):
    sub = iota((8, 128), 0)
    width = len(panel[0])
    for s in range(0, 4, SPAN):
        mine = range(s, s + SPAN)
        own = [list(panel[a]) for a in mine]
        count = 8 * SPAN
        cols = [[lane_spread(rows[0], base + 8 * s + c) for rows in own] for c in range(count)]
        inverses = []
        for j in range(0, count, 2):
            group, line = divmod(j, 8)
            corner = row_spread(cols[j][group], line)
            beside = row_spread(cols[j + 1][group], line)
            below = row_spread(cols[j][group], line + 1)
            last = row_spread(cols[j + 1][group], line + 1)
            first_inverse = 1.0 / corner
            ratio = below * first_inverse
            second_inverse = 1.0 / (last - ratio * beside)
            inverses += [first_inverse, second_inverse]
            first = [cols[j][a] * first_inverse for a in range(SPAN)]
            first[group] = jnp.where(sub == line, 0.0, first[group])
            second = [(cols[j + 1][a] - first[a] * beside) * second_inverse for a in range(SPAN)]
            second[group] = jnp.where(sub == line + 1, 0.0, second[group])

            def reduced(blocks):
                upper = row_spread(blocks[group], line)
                lower = row_spread(blocks[group], line + 1) - ratio * upper
                return [(blocks[a] - first[a] * upper) - second[a] * lower for a in range(SPAN)]

            for c in range(j + 2, count):
                cols[c] = reduced(cols[c])
            for t in range(width):
                for a, block in enumerate(reduced([rows[t] for rows in own])):
                    own[a][t] = block
        for a in range(SPAN):
            scale = inverses[8 * a]
            for line in range(1, 8):
                scale = jnp.where(sub == line, inverses[8 * a + line], scale)
            own[a] = [block * scale for block in own[a]]
        for a, rows in zip(mine, own):
            panel[a] = rows
        spread = [[row_spread(own[c // 8][t], c % 8) for c in range(count)] for t in range(width)]
        for a in range(len(panel)):
            if a in mine:
                continue
            factors = [lane_spread(panel[a][0], base + 8 * s + c) for c in range(count)]
            panel[a] = [
                panel[a][t] - total_of([factors[c] * spread[t][c] for c in range(count)]) for t in range(width)
            ]
    return panel


def eliminate(work):
    for q in range(NS // 32):
        half, base = q // 4, 32 * (q % 4)
        lanes = [slice(t * 128, (t + 1) * 128) for t in range(half, 3)]
        near = [2 * q, 2 * q + 1] + [2 * q + 2] * (q + 1 < NS // 32)
        rows = [slice(n * 16 + 8 * a, n * 16 + 8 * a + 8) for n in near for a in range(2)]
        panel = eliminate_panel([[work[r, at] for at in lanes] for r in rows], base)
        for r, group in zip(rows, panel):
            for at, block in zip(lanes, group):
                work[r, at] = block
        solved = jnp.concatenate([jnp.concatenate(group, axis=1) for group in panel[:4]], axis=0)
        mh, mm, ml = (part.astype(F32) for part in parts_of(solved))
        zero = jnp.zeros_like(mh)
        right = jnp.concatenate([mh, mh, mh, mm, ml, mm, zero, zero], axis=0).astype(BF16)
        far = [n % 16 for n in range(2 * q + 3, 2 * q + 19) if n % 16 not in near]
        subtract_panel(work, far, lanes, base, right)


def subtract_panel(work, some, lanes, base, right):
    factor = jnp.concatenate([work[n * 16 : n * 16 + 16, lanes[0]] for n in some], axis=0)
    column = iota(factor.shape, 1)
    factor = jnp.where((column >= base) & (column < base + 32), factor, 0.0)
    factor = pltpu.roll(factor, (128 - base) % 128, 1) if base else factor
    fh, fm, fl = (part.astype(F32) for part in parts_of(factor))
    pair = fh + pltpu.roll(fm, 32, 1)
    left = pair + pltpu.roll(fl, 64, 1) + pltpu.roll(fh, 96, 1)
    left = jnp.concatenate([left.astype(BF16), pair.astype(BF16)], axis=1)
    change = jnp.dot(left, right, preferred_element_type=F32)
    for m, n in enumerate(some):
        for t, at in enumerate(lanes):
            part = change[m * 16 : m * 16 + 16, t * 128 : (t + 1) * 128]
            work[n * 16 : n * 16 + 16, at] = work[n * 16 : n * 16 + 16, at] - part


def finish_update(shift_ref, gram_ref, cent_ref, out_ref, work):
    row = iota((HALF, HALF), 0)
    col = iota((HALF, HALF), 1)
    low = slice(0, HALF)
    high = slice(HALF, NS)
    first, second, cross = (gram_ref[:, 8 * n : 8 * n + 8, :].reshape(HALF, HALF) for n in range(3))
    diagonal = jnp.where(row == col, first + second, 0.0)
    trace = jnp.sum(jnp.sum(diagonal, axis=0, keepdims=True), axis=1, keepdims=True)
    shift = shift_ref[0] * (trace * (1.0 / NS))
    work[low, low] = jnp.where(row == col, first + shift, first)
    work[high, high] = jnp.where(row == col, second + shift, second)
    work[high, low] = cross
    work[low, high] = cross.T
    energy_lane = TAPS * CI - 128
    eliminate(work)
    answer = work[:, NS + energy_lane : NS + energy_lane + 1]
    raw_step = jnp.sum(answer * cent_ref[...], axis=0, keepdims=True)
    square_sum = jnp.zeros((1, 1), F32)
    weighted = (
        answer[low] * first + 2.0 * answer[high] * cross,
        answer[high] * second,
    )
    for side, product in zip((low, high), weighted):
        flat = jnp.sum(jnp.where(row == col, jnp.broadcast_to(answer[side], (HALF, HALF)), 0.0), axis=0, keepdims=True)
        square_sum += jnp.sum(jnp.sum(product, axis=0, keepdims=True) * flat, axis=1, keepdims=True)
    update = -raw_step / jnp.sqrt(square_sum / PARAMS + 1e-06)
    out_ref[...] = update[:, 0 : TAPS * CI]


def local_rows(
    words_ref, sector_ref, energy_ref, w_ref, bias_ref, readout_ref, feature_copies,
    rows_ref, f0, fp, fm, wb, cot, word_row,
):
    weight = w_ref[...]
    source_row = iota((TAPS * CI, CH), 0)
    lane_in = iota((TAPS * CI, CH), 1)
    same = iota((CH, CH), 0) // CI % 4 == iota((CH, CH), 1) // CI % 4
    for pair in range(4):
        wanted = lane_in % CI + (2 * pair + lane_in // HALF) * CI
        spread = (source_row == wanted).astype(F32).astype(BF16)
        block = lax.dot_general(weight, spread, (((0,), (0,)), ((), ())), preferred_element_type=F32)
        wb[pair] = jnp.where(same, block, 0.0).astype(BF16)

    word_row[...] = jnp.zeros_like(word_row)
    word_row[:, 0:77] = words_ref[...]
    bits = (jnp.broadcast_to(word_row[...], (32, 128)) >> iota((32, 128), 0)) & 1
    bits = bits.astype(F32).astype(BF16)
    site = iota((1, SITES), 1)
    word_of = site // 30
    bit_of = site - 30 * word_of
    pick_word = (iota((128, SITES), 0) == jnp.broadcast_to(word_of, (128, SITES))).astype(F32).astype(BF16)
    spread_bits = jnp.dot(bits, pick_word, preferred_element_type=F32)
    pick_bit = iota((32, SITES), 0) == jnp.broadcast_to(bit_of, (32, SITES))
    sign = 2.0 * jnp.sum(jnp.where(pick_bit, spread_bits, 0.0), axis=0, keepdims=True) - 1.0

    sector = sector_ref[0]
    wave_row = sector // SIDE
    wave_col = sector - wave_row * SIDE
    site_i = site // SIDE
    site_j = site - SIDE * site_i
    wave_arg = (wave_row * site_i + wave_col * site_j) % SIDE
    phase = jnp.cos(2.0 * math.pi / SIDE * wave_arg.astype(F32))

    bias = column_of(bias_ref[...])
    readout = column_of(readout_ref[...])

    for copy in feature_copies:
        copy.wait()
    for row in range(SIDE + 2):
        rows = pl.ds(row * SIDE, SIDE)
        wide = f0[rows, :].astype(F32)
        fp[rows, :] = pltpu.roll(wide, SIDE - 1, 0).astype(BF16)
        fm[rows, :] = pltpu.roll(wide, 1, 0).astype(BF16)

    held = (f0, fp, fm)
    for t in range(SITES // TILE):
        start = t * TILE
        preact = [bias[:HALF] * sign[:, start : start + TILE], bias[HALF:] * sign[:, start : start + TILE]]
        for n in range(2):
            half = slice(n * HALF, n * HALF + HALF)
            for pair, taps in enumerate(((0, 1), (2, 3), (4, 5), (6,))):
                patch = jnp.concatenate(
                    [
                        held[which][pl.ds(SIDE + start + shift * SIDE, TILE), half]
                        for which, shift in (SOURCES[k] for k in taps)
                    ],
                    axis=1,
                )
                weight = wb[pair, half, 0 : HALF * len(taps)]
                preact[n] += lax.dot_general(
                    weight, patch, (((1,), (1,)), ((), ())), preferred_element_type=F32
                )
        preact = jnp.concatenate(preact, axis=0)
        logistic = 0.5 + 0.5 * jnp.tanh(0.5 * preact)
        scale = readout * phase[:, start : start + TILE]
        value = scale * logistic * (1.0 + preact * (1.0 - logistic))
        cot[:, start : start + TILE] = value.astype(BF16)

    group = iota((HALF, HALF), 0) // CI
    lane = iota((HALF, HALF), 1)
    same_half = group == lane // CI
    spare = lane - CI * ((group + TAPS) % 4)
    energy = jnp.full((HALF, HALF), energy_ref[0], F32)
    high, middle, low = (part.astype(F32) for part in parts_of(energy))
    spare = jnp.where(spare == 0, high, jnp.where(spare == 1, middle, jnp.where(spare == 2, low, 0.0)))
    for n in range(2):
        half = slice(n * HALF, n * HALF + HALF)
        tiles = [jnp.zeros((HALF, HALF), F32), spare]
        for taps in ((0, 1), (2, 3), (4, 5), (6,)):
            patch = jnp.concatenate(
                [held[which][pl.ds(SIDE + shift * SIDE, SITES), half] for which, shift in (SOURCES[k] for k in taps)],
                axis=1,
            )
            block = jnp.dot(cot[half, :], patch, preferred_element_type=F32)
            for m, k in enumerate(taps):
                piece = jnp.where(same_half, block[:, m * HALF : m * HALF + HALF], 0.0)
                tiles[k // 4] += pltpu.roll(piece, (k % 4) * CI, 1) if k % 4 else piece
        rows_ref[n * 8 : n * 8 + 8] = jnp.concatenate(tiles, axis=1).astype(BF16).reshape(8, G, CH)


def farthest_first(distance):
    pairs = [(a, b) for a in range(4) for b in range(4) if a or b]
    return sorted(pairs, key=lambda pair: -distance(*pair))


def update_kernel(
    words_hbm, sector_hbm, energy_hbm, shift_hbm, w_hbm, bias_hbm, readout_hbm, feat_hbm,
    out_ref,
    words_ref, sector_ref, energy_ref, shift_ref, w_ref, bias_ref, readout_ref,
    f0, fp, fm, wb, cot, word_row, rows_ref,
    recv1, send2, recv2, part, sums, wide, gram_ref, cent_ref, work, copy_sems, send_sems, recv_sems,
):
    samp = lax.axis_index("samp")
    tile = lax.axis_index("tile")
    h = samp // 4
    l = (samp - h * 4) * 4 + tile
    l_samp = samp - h * 4

    def peer_h(other):
        return (other * 4 + l_samp, tile)

    def peer_l(other):
        return (h * 4 + other // 4, lax.rem(other, 4))

    y, z_high, inner = h // 4, lax.rem(h, 4), l // 4
    steps_h = farthest_first(lambda a, b: min(a, 4 - a) + 2 * min(b, 4 - b))
    others_h = [lax.rem(y + a, 4) * 4 + lax.rem(z_high + b, 4) for a, b in steps_h]
    steps_l = farthest_first(lambda a, b: a // 2 + min(b, 4 - b))
    others_l = [lax.bitwise_xor(inner, a) * 4 + lax.rem(tile + b, 4) for a, b in steps_l]

    barrier = pltpu.get_barrier_semaphore()
    for other in others_h:
        pl.semaphore_signal(barrier, inc=1, device_id=peer_h(other), device_id_type=pl.DeviceIdType.MESH)

    feature_copies = (
        pltpu.make_async_copy(feat_hbm, f0.at[pl.ds(SIDE, SITES)], copy_sems.at[0]),
        pltpu.make_async_copy(feat_hbm.at[pl.ds(SITES - SIDE, SIDE)], f0.at[pl.ds(0, SIDE)], copy_sems.at[1]),
        pltpu.make_async_copy(feat_hbm.at[pl.ds(0, SIDE)], f0.at[pl.ds(SIDE + SITES, SIDE)], copy_sems.at[2]),
    )
    pairs = (
        (w_hbm, w_ref), (words_hbm, words_ref), (bias_hbm, bias_ref),
        (readout_hbm, readout_ref), (sector_hbm, sector_ref), (energy_hbm, energy_ref), (shift_hbm, shift_ref),
    )
    small_copies = [pltpu.make_async_copy(a, b, copy_sems.at[3 + n]) for n, (a, b) in enumerate(pairs)]
    for copy in small_copies:
        copy.start()
    for copy in feature_copies:
        copy.start()
    for other in others_l:
        pl.semaphore_signal(barrier, inc=1, device_id=peer_l(other), device_id_type=pl.DeviceIdType.MESH)

    for copy in small_copies:
        copy.wait()
    local_rows(
        words_ref, sector_ref, energy_ref, w_ref, bias_ref, readout_ref, feature_copies,
        rows_ref, f0, fp, fm, wb, cot, word_row,
    )
    pl.semaphore_wait(barrier, 2 * (G - 1))

    def exchange(stage, mine, others, peer, source, target):
        for other in others:
            pltpu.make_async_remote_copy(
                src_ref=source(other),
                dst_ref=target.at[mine],
                send_sem=send_sems.at[stage],
                recv_sem=recv_sems.at[stage],
                device_id=peer(other),
                device_id_type=pl.DeviceIdType.MESH,
            ).start()

    def arrived(sems, stage, target):
        many = target.at[pl.ds(0, G - 1)]
        pltpu.make_async_copy(many, many, sems.at[stage]).wait()

    exchange(0, h, others_h, peer_h, lambda other: rows_ref.at[other], recv1)
    recv1[h] = rows_ref[h]
    turned_row = iota((NS, NS), 0)
    source_row = (turned_row % G) * G + turned_row // G
    turn = (iota((NS, NS), 1) == source_row).astype(F32).astype(BF16)
    group = samp // 8
    lane = iota((CH, CH), 1)
    moved = lane // HALF * HALF + (lane % HALF + group * CI) % HALF
    order = (iota((CH, CH), 0) == moved).astype(F32).astype(BF16)
    arrived(recv_sems, 0, recv1)
    turned = jnp.dot(turn, recv1[...].reshape(NS, CH), preferred_element_type=F32)
    send2[...] = turned.astype(BF16).reshape(G, G, CH)
    exchange(1, l, others_l, peer_l, lambda other: send2.at[other], recv2)
    recv2[l] = send2[l]
    arrived(recv_sems, 1, recv2)

    raw = jnp.dot(recv2[...].reshape(NS, CH), order, preferred_element_type=F32)
    mean = jnp.mean(raw, axis=0, keepdims=True)
    centered = jnp.where(lane < TAPS * CI, (raw - mean) * (1.0 / math.sqrt(NS)), 0.0)
    low, high = centered[:HALF], centered[HALF:]
    for n, (left, right) in enumerate(((low, low), (high, high), (high, low))):
        block = lax.dot_general(
            left, right, (((1,), (1,)), ((), ())), precision=HIGHEST, preferred_element_type=F32
        )
        part[:, 8 * n : 8 * n + 8, :] = block.reshape(G, 8, HALF)

    exchange(2, l, others_l, peer_l, lambda other: part.at[other], sums)
    sums[l] = part[l]
    energy = jnp.sum(jnp.where(lane >= TAPS * CI, raw, 0.0), axis=1, keepdims=True)
    cent_ref[...] = jnp.where(lane == TAPS * CI, energy, centered)
    arrived(recv_sems, 2, sums)
    wide[h] = jnp.sum(sums[...], axis=0)
    exchange(3, h, others_h, peer_h, lambda other: wide.at[h], wide)
    arrived(recv_sems, 3, wide)
    gram_ref[l] = jnp.sum(wide[...], axis=0)
    exchange(4, l, others_l, peer_l, lambda other: gram_ref.at[l], gram_ref)
    last = cent_ref[:, 128:256]
    work[:, NS : NS + 128] = jnp.where(iota((NS, 128), 1) == TAPS * CI - 128, last, 0.0)
    arrived(recv_sems, 4, gram_ref)
    finish_update(shift_ref, gram_ref, cent_ref, out_ref, work)
    for stage, sent in enumerate((recv1, recv2, sums, wide, gram_ref)):
        arrived(send_sems, stage, sent)


def update_of(features, spin_words, conv_weight, spin_bias, readout, sector, diag_shift, energy_dev):
    vmem = pl.BlockSpec(memory_space=pltpu.VMEM)
    hbm = pl.BlockSpec(memory_space=pltpu.HBM)
    small = pl.BlockSpec(memory_space=pl.ANY)
    return pl.pallas_call(
        update_kernel,
        out_shape=jax.ShapeDtypeStruct((1, TAPS * CI), F32),
        in_specs=[hbm, small, small, small, hbm, hbm, hbm, hbm],
        out_specs=vmem,
        scratch_shapes=[
            pltpu.VMEM((1, 77), jnp.int32),
            pltpu.SMEM((1,), jnp.int32),
            pltpu.SMEM((1,), F32),
            pltpu.SMEM((1,), F32),
            pltpu.VMEM((TAPS * CI, CH), BF16),
            pltpu.VMEM((1, CH), F32),
            pltpu.VMEM((1, CH), F32),
            pltpu.VMEM((PAD, CH), BF16),
            pltpu.VMEM((PAD, CH), BF16),
            pltpu.VMEM((PAD, CH), BF16),
            pltpu.VMEM((4, CH, CH), BF16),
            pltpu.VMEM((CH, SITES), BF16),
            pltpu.VMEM((1, 128), jnp.int32),
            pltpu.VMEM((G, G, CH), BF16),
            pltpu.VMEM((G, G, CH), BF16),
            pltpu.VMEM((G, G, CH), BF16),
            pltpu.VMEM((G, G, CH), BF16),
            pltpu.VMEM((G, 24, HALF), F32),
            pltpu.VMEM((G, 24, HALF), F32),
            pltpu.VMEM((G, 24, HALF), F32),
            pltpu.VMEM((G, 24, HALF), F32),
            pltpu.VMEM((NS, CH), F32),
            pltpu.VMEM((NS, NS + 128), F32),
            pltpu.SemaphoreType.DMA((10,)),
            pltpu.SemaphoreType.DMA((5,)),
            pltpu.SemaphoreType.DMA((5,)),
        ],
        compiler_params=pltpu.CompilerParams(
            collective_id=0, has_side_effects=True, vmem_limit_bytes=56 << 20
        ),
        name="update_of",
    )(
        spin_words, sector, energy_dev, diag_shift, conv_weight.T,
        spin_bias.reshape(1, CH), readout.reshape(1, CH), features.reshape(SITES, CH),
    )


def on_device(
    features, spin_words, conv_weight, spin_bias, readout, sector, diag_shift, energy_dev
):
    return update_of(
        features, spin_words, conv_weight, spin_bias, readout, sector, diag_shift, energy_dev
    )


def solution(mesh):
    placed = (
        P(("samp", "tile"), None, None, None),
        P(("samp", "tile"), None),
        P(),
        P(),
        P(),
        P(),
        P(),
        P(("samp", "tile")),
    )
    return jax.shard_map(
        on_device, mesh=mesh, in_specs=placed, out_specs=P(("samp", "tile"), None), check_vma=False
    )
```

```python
import functools
import math

import jax
import jax.numpy as jnp
from jax import lax
from jax.experimental import pallas as pl
from jax.experimental.pallas import tpu as pltpu
from jax.sharding import PartitionSpec as P

SIDE = 48
SITES = SIDE * SIDE
PAD = SITES + 2 * SIDE
CH = 256
CI = 32
TAPS = 7
PARAMS = CH * TAPS * CI
NS = 256
G = 16
SPAN = 2
HALF = NS // 2

SOURCES = ((0, 0), (0, 1), (0, -1), (1, 0), (2, 0), (2, 1), (1, -1))
TILE = 256
F32 = jnp.float32
BF16 = jnp.bfloat16
HIGHEST = lax.Precision.HIGHEST


def iota(shape, dim):
    return lax.broadcasted_iota(jnp.int32, shape, dim)


def column_of(row):
    shape = (CH, CH)
    picked = jnp.where(iota(shape, 0) == iota(shape, 1), jnp.broadcast_to(row, shape), 0.0)
    return jnp.sum(picked, axis=1, keepdims=True)


def parts_of(value):
    high = value.astype(BF16)
    rest = value - high.astype(F32)
    middle = rest.astype(BF16)
    low = (rest - middle.astype(F32)).astype(BF16)
    return high, middle, low


def row_spread(block, j):
    return jnp.broadcast_to(block[j : j + 1, :], (8, 128))


def lane_spread(block, j):
    return jnp.take_along_axis(block, jnp.full((8, 128), j, jnp.int32), axis=1)


def total_of(terms):
    while len(terms) > 1:
        odd = terms[-1:] if len(terms) % 2 else []
        terms = [a + b for a, b in zip(terms[::2], terms[1::2])] + odd
    return terms[0]


def eliminate_panel(panel, base):
    sub = iota((8, 128), 0)
    width = len(panel[0])
    for s in range(0, 4, SPAN):
        mine = range(s, s + SPAN)
        own = [list(panel[a]) for a in mine]
        count = 8 * SPAN
        cols = [[lane_spread(rows[0], base + 8 * s + c) for rows in own] for c in range(count)]
        inverses = []
        for j in range(0, count, 2):
            group, line = divmod(j, 8)
            corner = row_spread(cols[j][group], line)
            beside = row_spread(cols[j + 1][group], line)
            below = row_spread(cols[j][group], line + 1)
            last = row_spread(cols[j + 1][group], line + 1)
            first_inverse = 1.0 / corner
            ratio = below * first_inverse
            second_inverse = 1.0 / (last - ratio * beside)
            inverses += [first_inverse, second_inverse]
            first = [cols[j][a] * first_inverse for a in range(SPAN)]
            first[group] = jnp.where(sub == line, 0.0, first[group])
            second = [(cols[j + 1][a] - first[a] * beside) * second_inverse for a in range(SPAN)]
            second[group] = jnp.where(sub == line + 1, 0.0, second[group])

            def reduced(blocks):
                upper = row_spread(blocks[group], line)
                lower = row_spread(blocks[group], line + 1) - ratio * upper
                return [(blocks[a] - first[a] * upper) - second[a] * lower for a in range(SPAN)]

            for c in range(j + 2, count):
                cols[c] = reduced(cols[c])
            for t in range(width):
                for a, block in enumerate(reduced([rows[t] for rows in own])):
                    own[a][t] = block
        for a in range(SPAN):
            scale = inverses[8 * a]
            for line in range(1, 8):
                scale = jnp.where(sub == line, inverses[8 * a + line], scale)
            own[a] = [block * scale for block in own[a]]
        for a, rows in zip(mine, own):
            panel[a] = rows
        spread = [[row_spread(own[c // 8][t], c % 8) for c in range(count)] for t in range(width)]
        for a in range(len(panel)):
            if a in mine:
                continue
            factors = [lane_spread(panel[a][0], base + 8 * s + c) for c in range(count)]
            panel[a] = [
                panel[a][t] - total_of([factors[c] * spread[t][c] for c in range(count)]) for t in range(width)
            ]
    return panel


def eliminate(work):
    for q in range(NS // 32):
        half, base = q // 4, 32 * (q % 4)
        lanes = [slice(t * 128, (t + 1) * 128) for t in range(half, 3)]
        near = [2 * q, 2 * q + 1] + [2 * q + 2] * (q + 1 < NS // 32)
        rows = [slice(n * 16 + 8 * a, n * 16 + 8 * a + 8) for n in near for a in range(2)]
        panel = eliminate_panel([[work[r, at] for at in lanes] for r in rows], base)
        for r, group in zip(rows, panel):
            for at, block in zip(lanes, group):
                work[r, at] = block
        solved = jnp.concatenate([jnp.concatenate(group, axis=1) for group in panel[:4]], axis=0)
        mh, mm, ml = (part.astype(F32) for part in parts_of(solved))
        zero = jnp.zeros_like(mh)
        right = jnp.concatenate([mh, mh, mh, mm, ml, mm, zero, zero], axis=0).astype(BF16)
        far = [n % 16 for n in range(2 * q + 3, 2 * q + 19) if n % 16 not in near]
        for some in (far[:1], far[1:]):
            subtract_panel(work, some, lanes, base, right)


def subtract_panel(work, some, lanes, base, right):
    factor = jnp.concatenate([work[n * 16 : n * 16 + 16, lanes[0]] for n in some], axis=0)
    column = iota(factor.shape, 1)
    factor = jnp.where((column >= base) & (column < base + 32), factor, 0.0)
    factor = pltpu.roll(factor, (128 - base) % 128, 1) if base else factor
    fh, fm, fl = (part.astype(F32) for part in parts_of(factor))
    pair = fh + pltpu.roll(fm, 32, 1)
    left = pair + pltpu.roll(fl, 64, 1) + pltpu.roll(fh, 96, 1)
    left = jnp.concatenate([left.astype(BF16), pair.astype(BF16)], axis=1)
    change = jnp.dot(left, right, preferred_element_type=F32)
    for m, n in enumerate(some):
        for t, at in enumerate(lanes):
            part = change[m * 16 : m * 16 + 16, t * 128 : (t + 1) * 128]
            work[n * 16 : n * 16 + 16, at] = work[n * 16 : n * 16 + 16, at] - part


def finish_update(shift_ref, gram_ref, cent_ref, out_ref, work):
    row = iota((HALF, HALF), 0)
    col = iota((HALF, HALF), 1)
    low = slice(0, HALF)
    high = slice(HALF, NS)
    first, second, cross = (gram_ref[:, 8 * n : 8 * n + 8, :].reshape(HALF, HALF) for n in range(3))
    diagonal = jnp.where(row == col, first + second, 0.0)
    trace = jnp.sum(jnp.sum(diagonal, axis=0, keepdims=True), axis=1, keepdims=True)
    shift = shift_ref[0] * (trace * (1.0 / NS))
    work[low, low] = jnp.where(row == col, first + shift, first)
    work[high, high] = jnp.where(row == col, second + shift, second)
    work[high, low] = cross
    work[low, high] = cross.T
    energy_lane = TAPS * CI - 128
    eliminate(work)
    answer = work[:, NS + energy_lane : NS + energy_lane + 1]
    raw_step = jnp.sum(answer * cent_ref[...], axis=0, keepdims=True)
    square_sum = jnp.zeros((1, 1), F32)
    weighted = (
        answer[low] * first + 2.0 * answer[high] * cross,
        answer[high] * second,
    )
    for side, product in zip((low, high), weighted):
        flat = jnp.sum(jnp.where(row == col, jnp.broadcast_to(answer[side], (HALF, HALF)), 0.0), axis=0, keepdims=True)
        square_sum += jnp.sum(jnp.sum(product, axis=0, keepdims=True) * flat, axis=1, keepdims=True)
    update = -raw_step / jnp.sqrt(square_sum / PARAMS + 1e-06)
    out_ref[...] = update[:, 0 : TAPS * CI]


def local_rows(
    words_ref, sector_ref, energy_ref, w_ref, bias_ref, readout_ref, feature_copies,
    rows_ref, f0, fp, fm, wb, cot, word_row,
):
    weight = w_ref[...]
    source_row = iota((TAPS * CI, CH), 0)
    lane_in = iota((TAPS * CI, CH), 1)
    same = iota((CH, CH), 0) // CI % 4 == iota((CH, CH), 1) // CI % 4
    for pair in range(4):
        wanted = lane_in % CI + (2 * pair + lane_in // HALF) * CI
        spread = (source_row == wanted).astype(F32).astype(BF16)
        block = lax.dot_general(weight, spread, (((0,), (0,)), ((), ())), preferred_element_type=F32)
        wb[pair] = jnp.where(same, block, 0.0).astype(BF16)

    word_row[...] = jnp.zeros_like(word_row)
    word_row[:, 0:77] = words_ref[...]
    bits = (jnp.broadcast_to(word_row[...], (32, 128)) >> iota((32, 128), 0)) & 1
    bits = bits.astype(F32).astype(BF16)
    site = iota((1, SITES), 1)
    word_of = site // 30
    bit_of = site - 30 * word_of
    pick_word = (iota((128, SITES), 0) == jnp.broadcast_to(word_of, (128, SITES))).astype(F32).astype(BF16)
    spread_bits = jnp.dot(bits, pick_word, preferred_element_type=F32)
    pick_bit = iota((32, SITES), 0) == jnp.broadcast_to(bit_of, (32, SITES))
    sign = 2.0 * jnp.sum(jnp.where(pick_bit, spread_bits, 0.0), axis=0, keepdims=True) - 1.0

    sector = sector_ref[0]
    wave_row = sector // SIDE
    wave_col = sector - wave_row * SIDE
    site_i = site // SIDE
    site_j = site - SIDE * site_i
    wave_arg = (wave_row * site_i + wave_col * site_j) % SIDE
    phase = jnp.cos(2.0 * math.pi / SIDE * wave_arg.astype(F32))

    bias = column_of(bias_ref[...])
    readout = column_of(readout_ref[...])

    for copy in feature_copies:
        copy.wait()
    for row in range(SIDE + 2):
        rows = pl.ds(row * SIDE, SIDE)
        wide = f0[rows, :].astype(F32)
        fp[rows, :] = pltpu.roll(wide, SIDE - 1, 0).astype(BF16)
        fm[rows, :] = pltpu.roll(wide, 1, 0).astype(BF16)

    held = (f0, fp, fm)
    for t in range(SITES // TILE):
        start = t * TILE
        preact = [bias[:HALF] * sign[:, start : start + TILE], bias[HALF:] * sign[:, start : start + TILE]]
        for n in range(2):
            half = slice(n * HALF, n * HALF + HALF)
            for pair, taps in enumerate(((0, 1), (2, 3), (4, 5), (6,))):
                patch = jnp.concatenate(
                    [
                        held[which][pl.ds(SIDE + start + shift * SIDE, TILE), half]
                        for which, shift in (SOURCES[k] for k in taps)
                    ],
                    axis=1,
                )
                weight = wb[pair, half, 0 : HALF * len(taps)]
                preact[n] += lax.dot_general(
                    weight, patch, (((1,), (1,)), ((), ())), preferred_element_type=F32
                )
        preact = jnp.concatenate(preact, axis=0)
        logistic = 0.5 + 0.5 * jnp.tanh(0.5 * preact)
        scale = readout * phase[:, start : start + TILE]
        value = scale * logistic * (1.0 + preact * (1.0 - logistic))
        cot[:, start : start + TILE] = value.astype(BF16)

    group = iota((HALF, HALF), 0) // CI
    lane = iota((HALF, HALF), 1)
    same_half = group == lane // CI
    spare = lane - CI * ((group + TAPS) % 4)
    energy = jnp.full((HALF, HALF), energy_ref[0], F32)
    high, middle, low = (part.astype(F32) for part in parts_of(energy))
    spare = jnp.where(spare == 0, high, jnp.where(spare == 1, middle, jnp.where(spare == 2, low, 0.0)))
    for n in range(2):
        half = slice(n * HALF, n * HALF + HALF)
        tiles = [jnp.zeros((HALF, HALF), F32), spare]
        for taps in ((0, 1), (2, 3), (4, 5), (6,)):
            patch = jnp.concatenate(
                [held[which][pl.ds(SIDE + shift * SIDE, SITES), half] for which, shift in (SOURCES[k] for k in taps)],
                axis=1,
            )
            block = jnp.dot(cot[half, :], patch, preferred_element_type=F32)
            for m, k in enumerate(taps):
                piece = jnp.where(same_half, block[:, m * HALF : m * HALF + HALF], 0.0)
                tiles[k // 4] += pltpu.roll(piece, (k % 4) * CI, 1) if k % 4 else piece
        rows_ref[n * 8 : n * 8 + 8] = jnp.concatenate(tiles, axis=1).astype(BF16).reshape(8, G, CH)


def farthest_first(distance):
    pairs = [(a, b) for a in range(4) for b in range(4) if a or b]
    return sorted(pairs, key=lambda pair: -distance(*pair))


def update_kernel(
    words_hbm, sector_hbm, energy_hbm, shift_hbm, w_hbm, bias_hbm, readout_hbm, feat_hbm,
    out_ref,
    words_ref, sector_ref, energy_ref, shift_ref, w_ref, bias_ref, readout_ref,
    f0, fp, fm, wb, cot, word_row, rows_ref,
    recv1, send2, recv2, part, sums, wide, gram_ref, cent_ref, work, copy_sems, send_sems, recv_sems,
):
    samp = lax.axis_index("samp")
    tile = lax.axis_index("tile")
    h = samp // 4
    l = (samp - h * 4) * 4 + tile
    l_samp = samp - h * 4

    def peer_h(other):
        return (other * 4 + l_samp, tile)

    def peer_l(other):
        return (h * 4 + other // 4, lax.rem(other, 4))

    y, z_high, inner = h // 4, lax.rem(h, 4), l // 4
    steps_h = farthest_first(lambda a, b: min(a, 4 - a) + 2 * min(b, 4 - b))
    others_h = [lax.rem(y + a, 4) * 4 + lax.rem(z_high + b, 4) for a, b in steps_h]
    steps_l = farthest_first(lambda a, b: a // 2 + min(b, 4 - b))
    others_l = [lax.bitwise_xor(inner, a) * 4 + lax.rem(tile + b, 4) for a, b in steps_l]

    barrier = pltpu.get_barrier_semaphore()
    for other in others_h:
        pl.semaphore_signal(barrier, inc=1, device_id=peer_h(other), device_id_type=pl.DeviceIdType.MESH)

    feature_copies = (
        pltpu.make_async_copy(feat_hbm, f0.at[pl.ds(SIDE, SITES)], copy_sems.at[0]),
        pltpu.make_async_copy(feat_hbm.at[pl.ds(SITES - SIDE, SIDE)], f0.at[pl.ds(0, SIDE)], copy_sems.at[1]),
        pltpu.make_async_copy(feat_hbm.at[pl.ds(0, SIDE)], f0.at[pl.ds(SIDE + SITES, SIDE)], copy_sems.at[2]),
    )
    pairs = (
        (w_hbm, w_ref), (words_hbm, words_ref), (bias_hbm, bias_ref),
        (readout_hbm, readout_ref), (sector_hbm, sector_ref), (energy_hbm, energy_ref), (shift_hbm, shift_ref),
    )
    small_copies = [pltpu.make_async_copy(a, b, copy_sems.at[3 + n]) for n, (a, b) in enumerate(pairs)]
    for copy in small_copies:
        copy.start()
    for copy in feature_copies:
        copy.start()
    for other in others_l:
        pl.semaphore_signal(barrier, inc=1, device_id=peer_l(other), device_id_type=pl.DeviceIdType.MESH)

    for copy in small_copies:
        copy.wait()
    local_rows(
        words_ref, sector_ref, energy_ref, w_ref, bias_ref, readout_ref, feature_copies,
        rows_ref, f0, fp, fm, wb, cot, word_row,
    )
    pl.semaphore_wait(barrier, 2 * (G - 1))

    def exchange(stage, mine, others, peer, source, target):
        for other in others:
            pltpu.make_async_remote_copy(
                src_ref=source(other),
                dst_ref=target.at[mine],
                send_sem=send_sems.at[stage],
                recv_sem=recv_sems.at[stage],
                device_id=peer(other),
                device_id_type=pl.DeviceIdType.MESH,
            ).start()

    def arrived(sems, stage, target):
        many = target.at[pl.ds(0, G - 1)]
        pltpu.make_async_copy(many, many, sems.at[stage]).wait()

    exchange(0, h, others_h, peer_h, lambda other: rows_ref.at[other], recv1)
    recv1[h] = rows_ref[h]
    turned_row = iota((NS, NS), 0)
    source_row = (turned_row % G) * G + turned_row // G
    turn = (iota((NS, NS), 1) == source_row).astype(F32).astype(BF16)
    group = samp // 8
    lane = iota((CH, CH), 1)
    moved = lane // HALF * HALF + (lane % HALF + group * CI) % HALF
    order = (iota((CH, CH), 0) == moved).astype(F32).astype(BF16)
    arrived(recv_sems, 0, recv1)
    turned = jnp.dot(turn, recv1[...].reshape(NS, CH), preferred_element_type=F32)
    send2[...] = turned.astype(BF16).reshape(G, G, CH)
    exchange(1, l, others_l, peer_l, lambda other: send2.at[other], recv2)
    recv2[l] = send2[l]
    arrived(recv_sems, 1, recv2)

    raw = jnp.dot(recv2[...].reshape(NS, CH), order, preferred_element_type=F32)
    mean = jnp.mean(raw, axis=0, keepdims=True)
    centered = jnp.where(lane < TAPS * CI, (raw - mean) * (1.0 / math.sqrt(NS)), 0.0)
    low, high = centered[:HALF], centered[HALF:]
    for n, (left, right) in enumerate(((low, low), (high, high), (high, low))):
        block = lax.dot_general(
            left, right, (((1,), (1,)), ((), ())), precision=HIGHEST, preferred_element_type=F32
        )
        part[:, 8 * n : 8 * n + 8, :] = block.reshape(G, 8, HALF)

    exchange(2, l, others_l, peer_l, lambda other: part.at[other], sums)
    sums[l] = part[l]
    energy = jnp.sum(jnp.where(lane >= TAPS * CI, raw, 0.0), axis=1, keepdims=True)
    cent_ref[...] = jnp.where(lane == TAPS * CI, energy, centered)
    arrived(recv_sems, 2, sums)
    wide[h] = jnp.sum(sums[...], axis=0)
    exchange(3, h, others_h, peer_h, lambda other: wide.at[h], wide)
    arrived(recv_sems, 3, wide)
    gram_ref[l] = jnp.sum(wide[...], axis=0)
    exchange(4, l, others_l, peer_l, lambda other: gram_ref.at[l], gram_ref)
    last = cent_ref[:, 128:256]
    work[:, NS : NS + 128] = jnp.where(iota((NS, 128), 1) == TAPS * CI - 128, last, 0.0)
    arrived(recv_sems, 4, gram_ref)
    finish_update(shift_ref, gram_ref, cent_ref, out_ref, work)
    for stage, sent in enumerate((recv1, recv2, sums, wide, gram_ref)):
        arrived(send_sems, stage, sent)


def update_of(features, spin_words, conv_weight, spin_bias, readout, sector, diag_shift, energy_dev):
    vmem = pl.BlockSpec(memory_space=pltpu.VMEM)
    hbm = pl.BlockSpec(memory_space=pltpu.HBM)
    small = pl.BlockSpec(memory_space=pl.ANY)
    return pl.pallas_call(
        update_kernel,
        out_shape=jax.ShapeDtypeStruct((1, TAPS * CI), F32),
        in_specs=[hbm, small, small, small, hbm, hbm, hbm, hbm],
        out_specs=vmem,
        scratch_shapes=[
            pltpu.VMEM((1, 77), jnp.int32),
            pltpu.SMEM((1,), jnp.int32),
            pltpu.SMEM((1,), F32),
            pltpu.SMEM((1,), F32),
            pltpu.VMEM((TAPS * CI, CH), BF16),
            pltpu.VMEM((1, CH), F32),
            pltpu.VMEM((1, CH), F32),
            pltpu.VMEM((PAD, CH), BF16),
            pltpu.VMEM((PAD, CH), BF16),
            pltpu.VMEM((PAD, CH), BF16),
            pltpu.VMEM((4, CH, CH), BF16),
            pltpu.VMEM((CH, SITES), BF16),
            pltpu.VMEM((1, 128), jnp.int32),
            pltpu.VMEM((G, G, CH), BF16),
            pltpu.VMEM((G, G, CH), BF16),
            pltpu.VMEM((G, G, CH), BF16),
            pltpu.VMEM((G, G, CH), BF16),
            pltpu.VMEM((G, 24, HALF), F32),
            pltpu.VMEM((G, 24, HALF), F32),
            pltpu.VMEM((G, 24, HALF), F32),
            pltpu.VMEM((G, 24, HALF), F32),
            pltpu.VMEM((NS, CH), F32),
            pltpu.VMEM((NS, NS + 128), F32),
            pltpu.SemaphoreType.DMA((10,)),
            pltpu.SemaphoreType.DMA((5,)),
            pltpu.SemaphoreType.DMA((5,)),
        ],
        compiler_params=pltpu.CompilerParams(
            collective_id=0, has_side_effects=True, vmem_limit_bytes=56 << 20
        ),
        name="update_of",
    )(
        spin_words, sector, energy_dev, diag_shift, conv_weight.T,
        spin_bias.reshape(1, CH), readout.reshape(1, CH), features.reshape(SITES, CH),
    )


def on_device(
    features, spin_words, conv_weight, spin_bias, readout, sector, diag_shift, energy_dev
):
    return update_of(
        features, spin_words, conv_weight, spin_bias, readout, sector, diag_shift, energy_dev
    )


def solution(mesh):
    placed = (
        P(("samp", "tile"), None, None, None),
        P(("samp", "tile"), None),
        P(),
        P(),
        P(),
        P(),
        P(),
        P(("samp", "tile")),
    )
    return jax.shard_map(
        on_device, mesh=mesh, in_specs=placed, out_specs=P(("samp", "tile"), None), check_vma=False
    )
```
